128 devices in a mesh: req: 64 (over z, x, y), kv: 2 (over core).
Axes of the slice: x: 4, y: 4, z: 4, core: 2. Of those that a mesh axis runs over, the one named last changes fastest.
Arguments:
- tokens: bfloat16 [1024, 1536], P('req'), may hold values from -6 to 6
- gain_attn: bfloat16 [1536], replicated, may hold values from 0.099609375 to 1.8984375
- w_query: bfloat16 [1536, 1536], P(None, 'kv'), may hold values from -0.15625 to 0.15625
- w_key: bfloat16 [1536, 256], P(None, 'kv'), may hold values from -0.15625 to 0.15625
- w_value: bfloat16 [1536, 256], P(None, 'kv'), may hold values from -0.15625 to 0.15625
- w_out: bfloat16 [1536, 1536], P('kv'), may hold values from -0.15625 to 0.15625
- cache_k: bfloat16 [4096, 128, 256], P('req', None, 'kv'), may hold values from -720 to 720
- cache_v: bfloat16 [4096, 128, 256], P('req', None, 'kv'), may hold values from -6 to 6
- page_table: int32 [1024, 4], P('req'), may hold values from 0 to 63, as said below
- lengths: int32 [1024], replicated, may hold values from 1 to 512, as said below
- new_owner: int32 [64], replicated, may hold values from 0 to 63, as said below
- gain_moe: bfloat16 [1536], replicated, may hold values from 0.099609375 to 1.8984375
- w_router: bfloat16 [1536, 32], replicated, may hold values from -0.15625 to 0.15625
- routes: int32 [1024, 4], P(('req', 'kv')), may hold values from 0 to 31, all different within a row; in each aligned block of 8 rows (0 to 7, 8 to 15, ...) at most 2 rows name the same one
- w_gate: bfloat16 [64, 1536, 384], P('req', None, 'kv'), may hold values from -0.15625 to 0.15625
- w_up: bfloat16 [64, 1536, 384], P('req', None, 'kv'), may hold values from -0.15625 to 0.15625
- w_down: bfloat16 [64, 1536, 384], P('req', None, 'kv'), may hold values from -0.21875 to 0.21875
Outputs:
- layer_out: bfloat16 [1024, 1536], P(('req', 'kv'))
The draws below stay inside these ranges and needn't reach their ends.
Inputs may be any that keep to these rules, and one draw needn't show every extreme that they name: `lengths`: the last slot of each device (15, 31, ...) holds at most 256, and some last slot holds exactly 256; some length equals 512. `page_table`: the page indices of the 16 slots of one device are together a permutation of 0 to 63. `new_owner`: A permutation of the devices of req. `routes`: in each aligned block of 8 rows (the rows of one device) no expert is named by more than 2 rows.
All inputs are finite; a program needn't handle non-finite values.
Results may differ from the reference program's by a relative error of at most 0.015.
The reference program's roundings to bfloat16 on the way (of `normed`, `queries`, `attended`, `middle`, `normed_two` and `hidden`) count: a program that leaves them out, or rounds other values in their place, can miss the bound.
Values may be sent and summed in bfloat16 or wider, within the bound.
A program may use at most 128 MiB of HBM per device.

```python
import math
import jax
import jax.numpy as jnp
import numpy as np
from jax import lax

D = 1536
H = 12
KVH = 2
HD = 128
FF = 768
TOPK = 4
REQ_DEV = 16
PAGE = 128
MAXLEN = 512
MOVE_LEN = 256
EXPERTS = 32
ROWS_DEV = 8
REQS = 1024
PPR = 4
POOL_DEV = 64
POOL = 4096
CAP = 2


def draw_cache_k(key, part):
    key_base = jax.random.fold_in(key, 0)
    base = jax.random.normal(key_base, (POOL, PAGE, KVH * HD), jnp.float32)
    base = jnp.clip(base, -6.0, 6.0)
    return base.astype(jnp.bfloat16)


def draw_page_table(key, part):
    device_count = REQS // REQ_DEV
    key_list = jax.random.split(key, device_count)
    permuted = jax.vmap(lambda one_key: jax.random.permutation(one_key, POOL_DEV))(key_list)
    return permuted.reshape(REQS, PPR).astype(jnp.int32)


def draw_lengths(key, part):
    device_count = REQS // REQ_DEV
    key_cap, key_raw, key_moved = jax.random.split(key, 3)
    device_cap = jax.random.randint(key_cap, (device_count, 1), MAXLEN // 4, MAXLEN + 1)
    raw_draw = jax.random.randint(key_raw, (device_count, REQ_DEV), 0, 1 << 20)
    lengths_all = 1 + raw_draw % device_cap
    moved = 1 + jax.random.randint(key_moved, (device_count,), 0, MOVE_LEN)
    lengths_all = lengths_all.at[:, REQ_DEV - 1].set(moved)
    lengths_all = lengths_all.at[0, 0].set(MAXLEN).at[0, REQ_DEV - 1].set(MOVE_LEN)
    return lengths_all.reshape(REQS).astype(jnp.int32)


def place_value(perm, position, wanted):
    spots = jnp.arange(perm.shape[0], dtype=jnp.int32)
    where_now = jnp.sum(jnp.where(perm == wanted, spots, 0)).astype(jnp.int32)
    held = perm[position]
    perm = perm.at[where_now].set(held)
    return perm.at[position].set(wanted)


def draw_new_owner(key, part):
    device_count = REQS // REQ_DEV
    perm = jax.random.permutation(key, device_count).astype(jnp.int32)
    perm = place_value(perm, 0, 1)
    perm = place_value(perm, 1, 1 + device_count // 2)
    perm = place_value(perm, 3, 2)
    return perm.astype(jnp.int32)


def steps_of(stream_key, shape, pieces, least, high):
    def one(dim, parts):
        draws = jax.random.uniform(jax.random.fold_in(jax.random.fold_in(stream_key, 6), dim), (parts,), jnp.float32, least / len(pieces), high / len(pieces))
        return jnp.repeat(jnp.exp(draws), shape[dim] // parts).reshape((-1,) + (1,) * (len(shape) - dim - 1))

    loudness = one(*pieces[0])
    for cut in pieces[1:]:
        loudness = loudness * one(*cut)
    return loudness


def shared_out(rng, own, number, rows, count, top, reach, skew):
    ranking = jax.random.permutation(rng, count)
    packed, common = load_shares(count, rows * top, reach, skew, True), load_shares(count, rows * top, reach, skew, False)
    places = jnp.arange(count)

    def named(sizes, rotation):
        used = int((sizes > 0).sum())
        fixed = max(1, used // 4)
        shifted = fixed + (places - fixed + rotation * (used - fixed)) % max(1, count - fixed)
        return jnp.zeros((count,), jnp.int32).at[ranking[jnp.where(places < fixed, places, shifted)]].set(jnp.asarray(sizes, jnp.int32))

    sizes = jnp.where(number % 4 == 0, named(packed, number // 4), named(common, number - number // 4 - 1))
    mixed = jax.random.permutation(jax.random.fold_in(own, 3), count)
    donor, taker = mixed[0:count // 2 * 2:2], mixed[1:count // 2 * 2:2]
    room = jnp.minimum(sizes[donor] - 1, reach - sizes[taker]) // 2
    room = jnp.where((donor == ranking[0]) | (taker == ranking[0]) | (sizes[taker] == 0), 0, jnp.maximum(room, 0))
    shifted = jax.random.randint(jax.random.fold_in(own, 4), (count // 2,), 0, 1 << 20) % (room + 1)
    sizes = sizes.at[donor].add(-shifted).at[taker].add(shifted)
    items = jnp.searchsorted(jnp.cumsum(sizes), jnp.arange(rows * top), side="right").astype(jnp.int32)
    table = items.reshape(top, rows).T
    table = table[jax.random.permutation(jax.random.fold_in(own, 1), rows)]
    rotation = jax.random.randint(jax.random.fold_in(own, 2), (rows, 1), 0, top)
    return jnp.take_along_axis(table, (jnp.arange(top)[None, :] + rotation) % top, axis=1)


def load_shares(amount, total, most, skew, full):
    portions = [(1 << 20) // math.isqrt(grade ** skew) + 1 for grade in range(1, amount + 1)]
    largest = most if full else min(most, max(-(-total // amount), total * portions[0] // sum(portions)))
    least = 1 if total - largest >= amount - 1 else 0
    counts, surplus = [largest] + [least] * (amount - 1), total - largest - least * (amount - 1)
    while surplus > 0:
        candidates = [i for i in range(1, amount) if counts[i] < largest] or [i for i in range(1, amount) if counts[i] < most]
        mass, remaining = sum([portions[i] for i in candidates]), surplus
        for i in candidates:
            more = min(most - counts[i], max(1, remaining * portions[i] // mass), surplus)
            counts[i] = counts[i] + more
            surplus = surplus - more
    return np.array(counts)


def gaussian(stream_key, extent, scale, limit, cuts=(), kind=jnp.bfloat16):
    entries = scale * jax.random.normal(stream_key, extent, jnp.float32)
    if cuts:
        entries = entries * steps_of(stream_key, extent, cuts, -0.22, 0.18)
    return jnp.clip(entries, -limit, limit).astype(kind)


def setup_inputs(seed: int = 0) -> dict:
    seeds = jax.random.split(jax.random.key(seed), 18)
    tokens = gaussian(seeds[0], (REQS, D), 1.0, 6.0, ((0, 64),))
    gain_attn = jnp.clip(1.0 + 0.18 * jax.random.normal(seeds[1], (D,), jnp.float32), 0.099609375, 1.8984375).astype(jnp.bfloat16)
    w_query = gaussian(seeds[2], (D, H * HD), D ** -0.5, 0.15625, ((1, 2),))
    w_key = gaussian(seeds[3], (D, KVH * HD), D ** -0.5, 0.15625, ((1, 2),))
    w_value = gaussian(seeds[4], (D, KVH * HD), D ** -0.5, 0.15625, ((1, 2),))
    w_out = gaussian(seeds[5], (H * HD, D), (H * HD) ** -0.5, 0.15625, ((0, 2),))
    cache_k = draw_cache_k(jax.random.fold_in(seeds[17], 71), 0)
    cache_v = gaussian(seeds[7], (POOL, PAGE, KVH * HD), 1.0, 6.0, ((0, 64), (2, 2)))
    page_table = draw_page_table(jax.random.fold_in(seeds[17], 71), 0)
    lengths = draw_lengths(jax.random.fold_in(seeds[17], 71), 0)
    new_owner = draw_new_owner(jax.random.fold_in(seeds[17], 71), 0)
    gain_moe = jnp.clip(1.0 + 0.18 * jax.random.normal(seeds[11], (D,), jnp.float32), 0.099609375, 1.8984375).astype(jnp.bfloat16)
    w_router = gaussian(seeds[12], (D, EXPERTS), D ** -0.5, 0.15625)
    routes_keys = jax.random.split(jax.random.fold_in(seeds[13], 1), REQS // ROWS_DEV)
    routes_turns = jax.random.permutation(jax.random.fold_in(seeds[13], 3), REQS // ROWS_DEV)
    routes = jax.vmap(lambda own, number: shared_out(jax.random.fold_in(seeds[13], 2), own, number, ROWS_DEV, EXPERTS, TOPK, CAP, 2))(routes_keys, routes_turns).reshape((REQS, TOPK))
    w_gate = gaussian(seeds[14], (2 * EXPERTS, D, FF // 2), D ** -0.5, 0.15625, ((0, 64), (2, 2)))
    w_up = gaussian(seeds[15], (2 * EXPERTS, D, FF // 2), D ** -0.5, 0.15625, ((0, 64), (2, 2)))
    w_down = gaussian(seeds[16], (2 * EXPERTS, D, FF // 2), FF ** -0.5, 0.21875, ((0, 64), (2, 2)))
    return dict(tokens=tokens, gain_attn=gain_attn, w_query=w_query, w_key=w_key, w_value=w_value, w_out=w_out, cache_k=cache_k, cache_v=cache_v, page_table=page_table, lengths=lengths, new_owner=new_owner, gain_moe=gain_moe, w_router=w_router, routes=routes, w_gate=w_gate, w_up=w_up, w_down=w_down)


def rms_scaled(values, gain_vec):
    wide = values.astype(jnp.float32)
    squares = lax.optimization_barrier(jnp.mean(wide * wide, axis=-1, keepdims=True))
    return (wide * lax.rsqrt(squares + 1e-06) * gain_vec.astype(jnp.float32)).astype(jnp.bfloat16)

def reference(tokens, gain_attn, w_query, w_key, w_value, w_out, cache_k, cache_v, page_table, lengths, new_owner, gain_moe, w_router, routes, w_gate, w_up, w_down):
    device_count = REQS // REQ_DEV
    groups = H // KVH
    inv_root = HD ** (-0.5)
    inverse = jnp.zeros((device_count,), jnp.int32).at[new_owner].set(jnp.arange(device_count, dtype=jnp.int32))
    slot_ids = jnp.arange(REQS, dtype=jnp.int32)
    home_device = slot_ids // REQ_DEV
    source = jnp.where(slot_ids % REQ_DEV == REQ_DEV - 1, inverse[home_device] * REQ_DEV + REQ_DEV - 1, slot_ids).astype(jnp.int32)
    normed = rms_scaled(tokens, gain_attn)
    queries = jnp.dot(normed, w_query, preferred_element_type=jnp.float32).astype(jnp.bfloat16).reshape(REQS, KVH, groups, HD)
    keys_new = jnp.dot(normed, w_key, preferred_element_type=jnp.float32).astype(jnp.bfloat16).reshape(REQS, KVH, HD)
    values_new = jnp.dot(normed, w_value, preferred_element_type=jnp.float32).astype(jnp.bfloat16).reshape(REQS, KVH, HD)
    live_lengths = lengths[source]

    def attend(request_item):
        query_row, key_now, value_now, anchor, live_len = request_item
        pool_rows = anchor // REQ_DEV * POOL_DEV + page_table[anchor]
        page_keys = cache_k[pool_rows].reshape(MAXLEN, KVH, HD).astype(jnp.float32)
        page_values = cache_v[pool_rows].reshape(MAXLEN, KVH, HD).astype(jnp.float32)
        query_f = query_row.astype(jnp.float32)
        scores = jnp.einsum('kgd,tkd->kgt', query_f, page_keys) * inv_root
        live_mask = jnp.arange(MAXLEN, dtype=jnp.int32)[None, None, :] < live_len
        scores = jnp.where(live_mask, scores, -1e+30)
        top_score = lax.optimization_barrier(jnp.max(scores, axis=-1))
        weights = jnp.where(live_mask, jnp.exp(scores - top_score[..., None]), 0.0)
        totals = lax.optimization_barrier(jnp.sum(weights, axis=-1))
        accumulated = jnp.einsum('kgt,tkd->kgd', weights.astype(jnp.bfloat16).astype(jnp.float32), page_values)
        own_score = jnp.einsum('kgd,kd->kg', query_f, key_now.astype(jnp.float32)) * inv_root
        joint_max = jnp.maximum(top_score, own_score)
        old_part = jnp.exp(top_score - joint_max)
        new_part = jnp.exp(own_score - joint_max)
        merged = accumulated * old_part[..., None] + new_part[..., None] * value_now.astype(jnp.float32)[:, None, :]
        result = merged / (totals * old_part + new_part)[..., None]
        return result.astype(jnp.bfloat16).reshape(H * HD)
    attended = lax.map(attend, (queries, keys_new, values_new, source, live_lengths))
    middle = (tokens.astype(jnp.float32) + jnp.dot(attended, w_out, preferred_element_type=jnp.float32)).astype(jnp.bfloat16)
    normed_two = rms_scaled(middle, gain_moe)
    logits = jnp.dot(normed_two, w_router, preferred_element_type=jnp.float32)
    route_weight = jax.nn.softmax(jnp.take_along_axis(logits, routes, axis=1), axis=-1)
    block_count = REQS // ROWS_DEV
    per_block = ROWS_DEV * TOPK
    flat_routes = routes.reshape(block_count, per_block)
    onehot = (flat_routes[..., None] == jnp.arange(EXPERTS, dtype=jnp.int32)).astype(jnp.int32)
    slot_rank = lax.optimization_barrier(jnp.sum((jnp.cumsum(onehot, axis=1) - onehot) * onehot, axis=-1))
    block_ids = jnp.arange(block_count, dtype=jnp.int32)[:, None]
    row_ids = block_ids * ROWS_DEV + jnp.arange(per_block, dtype=jnp.int32)[None, :] // TOPK
    slot_spot = block_ids * CAP + slot_rank
    row_table = jnp.zeros((EXPERTS, block_count * CAP), jnp.int32).at[flat_routes, slot_spot].set(row_ids)
    scale_table = jnp.zeros((EXPERTS, block_count * CAP), jnp.float32).at[flat_routes, slot_spot].set(route_weight.reshape(block_count, per_block))
    gate_pairs = w_gate.reshape(EXPERTS, 2, D, FF // 2)
    up_pairs = w_up.reshape(EXPERTS, 2, D, FF // 2)
    down_pairs = w_down.reshape(EXPERTS, 2, D, FF // 2)

    def run_expert(expert_item):
        index_rows, weight_rows, gate_pair, up_pair, down_pair = expert_item
        inputs = normed_two[index_rows]
        gate_full = jnp.concatenate([gate_pair[0], gate_pair[1]], axis=1)
        up_full = jnp.concatenate([up_pair[0], up_pair[1]], axis=1)
        down_full = jnp.concatenate([down_pair[0], down_pair[1]], axis=1)
        gate_val = jnp.dot(inputs, gate_full, preferred_element_type=jnp.float32)
        up_val = jnp.dot(inputs, up_full, preferred_element_type=jnp.float32)
        hidden = (jax.nn.relu(gate_val) * up_val).astype(jnp.bfloat16)
        outputs = lax.dot_general(hidden, down_full, (((1,), (1,)), ((), ())), preferred_element_type=jnp.float32)
        return outputs * weight_rows[:, None]
    contrib = lax.map(run_expert, (row_table, scale_table, gate_pairs, up_pairs, down_pairs))
    mixed = jnp.zeros((REQS, D), jnp.float32).at[row_table.reshape(-1)].add(contrib.reshape(-1, D))
    return (middle.astype(jnp.float32) + mixed).astype(jnp.bfloat16)
```

```python
import functools

import jax
import jax.numpy as jnp
from jax import lax
from jax.experimental import pallas as pl
from jax.experimental.pallas import tpu as pltpu
from jax.sharding import PartitionSpec as P

BF = jnp.bfloat16
F32 = jnp.float32
LAST = (((1,), (1,)), ((), ()))


def rms_scaled(wide, gain_row):
    squares = jnp.mean(wide * wide, axis=-1, keepdims=True)
    return (wide * lax.rsqrt(squares + 1e-06) * gain_row).astype(BF)


def wait_bytes(ref, sem):
    pltpu.make_async_copy(ref, ref, sem).wait()


def layer_kernel(
    n,
    pages_s,
    lengths_s,
    owner_s,
    routes_s,
    tokens_h,
    gains_h,
    wq_h,
    wk_h,
    wv_h,
    wo_h,
    ck_h,
    cv_h,
    wr_h,
    wg_h,
    wu_h,
    wd_h,
    out_ref,
    tok,
    gains,
    wqkv,
    wo,
    ck,
    cv,
    wr,
    wg,
    wu,
    wd,
    heads,
    scores,
    att,
    q_out,
    q_in,
    a_out,
    a_in,
    head_sum,
    head_in,
    wide_a,
    disp_out,
    disp_in,
    wide_b,
    ret_out,
    ret_in,
    load_sems,
    w_send,
    w_recv,
    h_send,
    h_recv,
    send_sems,
    recv_sems,
):
    me = lax.axis_index("req")
    kv = lax.axis_index("kv")
    slots, width = tok.shape
    half = slots // 2
    hd = ck.shape[2]
    page = ck.shape[1]
    per_slot = pages_s.shape[0]
    groups = wo.shape[0] // hd
    experts = n // 2
    cols = width // hd
    inv_root = hd ** (-0.5)

    def load(src, dst, i):
        copy = pltpu.make_async_copy(src, dst, load_sems.at[i])
        copy.start()
        return copy

    qcols = wq_h.shape[1]
    l_tok = load(tokens_h, tok, 0)
    l_gain = load(gains_h, gains, 1)
    l_wq = load(wq_h, wqkv.at[:, pl.ds(0, qcols)], 2)
    l_wk = load(wk_h, wqkv.at[:, pl.ds(qcols, hd)], 3)
    l_wv = load(wv_h, wqkv.at[:, pl.ds(qcols + hd, hd)], 4)
    l_ck = load(ck_h, ck, 5)
    l_cv = load(cv_h, cv, 6)
    l_wo = load(wo_h, wo, 7)
    l_wr = load(wr_h, wr, 8)
    l_wg = load(wg_h.at[0], wg.at[0], 9)
    l_wu = load(wu_h.at[0], wu.at[0], 10)
    l_wd = load(wd_h.at[0], wd.at[0], 11)

    barrier = pltpu.get_barrier_semaphore()

    def greet(i, carry):
        pl.semaphore_signal(barrier, 1, device_id={"req": lax.rem(me + i, n)})
        return carry

    pl.semaphore_signal(barrier, 1, device_id={"kv": 1 - kv})
    lax.fori_loop(1, n, greet, 0)

    def to_all(src_of, dst, phase):
        def send(i, carry):
            peer = lax.rem(me + i, n)
            pltpu.make_async_remote_copy(
                src_ref=src_of(peer),
                dst_ref=dst.at[me],
                send_sem=send_sems.at[phase],
                recv_sem=recv_sems.at[phase],
                device_id={"req": peer},
            ).start()
            return carry

        pltpu.make_async_copy(src_of(me), dst.at[me], recv_sems.at[phase]).start()
        lax.fori_loop(1, n, send, 0)

    l_tok.wait()
    l_gain.wait()
    tokf = tok[...].astype(F32)
    normed = rms_scaled(tokf, gains[0:1, :])
    l_wq.wait()
    l_wk.wait()
    l_wv.wait()
    qkv = jnp.dot(normed, wqkv[...], preferred_element_type=F32).astype(BF).astype(F32)
    for h in range(groups + 2):
        heads[pl.ds(h, slots, stride=8), :] = qkv[:, h * hd : (h + 1) * hd]
    last = (slots - 1) * 8
    q_out[...] = heads[last : last + 8, :].astype(BF)

    pl.semaphore_wait(barrier, n)
    to_all(lambda peer: q_out, q_in, 0)
    sibling = {"kv": 1 - kv}
    swaps = []
    for i, (src, dst) in enumerate(((wg_h, wg), (wu_h, wu), (wd_h, wd))):
        swap = pltpu.make_async_remote_copy(
            src_ref=src.at[0],
            dst_ref=dst.at[1],
            send_sem=w_send.at[i],
            recv_sem=w_recv.at[i],
            device_id=sibling,
        )
        swap.start()
        swaps.append(swap)

    def attend(first, count):
        rows = slice(first * 8, (first + count) * 8)
        place = lax.broadcasted_iota(jnp.int32, (8, page), 1)
        for s in range(first, first + count):
            block = heads[s * 8 : s * 8 + 8, :].astype(BF)
            live = lengths_s[me * slots + s]
            for j in range(per_slot):
                dots = lax.dot_general(
                    block, ck[pages_s[j, s]], LAST, preferred_element_type=F32
                )
                scores[s * 8 : s * 8 + 8, j * page : (j + 1) * page] = jnp.where(
                    place + j * page < live, dots * inv_root, -1e30
                )
        all_scores = scores[rows, :]
        top = jnp.max(all_scores, axis=-1, keepdims=True)
        weights = jnp.exp(all_scores - top)
        total = jnp.sum(weights, axis=-1, keepdims=True)
        scores[rows, :] = weights
        for s in range(first, first + count):
            acc = jnp.zeros((8, hd), F32)
            for j in range(per_slot):
                acc = acc + jnp.dot(
                    scores[s * 8 : s * 8 + 8, j * page : (j + 1) * page].astype(BF),
                    cv[pages_s[j, s]],
                    preferred_element_type=F32,
                )
            att[s * 8 : s * 8 + 8, :] = acc
        block = heads[rows, :].reshape(count, 8, hd)
        own = jnp.sum(block * block[:, groups : groups + 1, :], axis=-1, keepdims=True) * inv_root
        top = top.reshape(count, 8, 1)
        total = total.reshape(count, 8, 1)
        joint = jnp.maximum(top, own)
        old_part = jnp.exp(top - joint)
        new_part = jnp.exp(own - joint)
        merged = (
            att[rows, :].reshape(count, 8, hd) * old_part
            + new_part * block[:, groups + 1 : groups + 2, :]
        )
        result = merged / (total * old_part + new_part)
        att[rows, :] = result.astype(BF).astype(F32).reshape(count * 8, hd)

    l_ck.wait()
    l_cv.wait()
    attend(0, slots - 1)

    wait_bytes(q_in, recv_sems.at[0])
    heads[last : last + 8, :] = q_in[owner_s[me]].astype(F32)
    attend(slots - 1, 1)
    a_out[...] = att[last : last + 8, :].astype(BF)
    to_all(lambda peer: a_out, a_in, 1)

    def find(c, found):
        return jnp.where(owner_s[c] == me, c, found)

    origin = lax.fori_loop(0, n, find, 0)
    l_wo.wait()
    wait_bytes(a_in, recv_sems.at[1])
    att[last : last + 8, :] = a_in[origin].astype(F32)
    attended = jnp.concatenate(
        [att[pl.ds(h, slots, stride=8), :].astype(BF) for h in range(groups)], axis=1
    )
    terms = jnp.dot(attended, wo[...], preferred_element_type=F32)
    head_sum[0] = terms[:half]
    head_sum[1] = terms[half:]
    cross = pltpu.make_async_remote_copy(
        src_ref=head_sum.at[1 - kv],
        dst_ref=head_in,
        send_sem=h_send,
        recv_sem=h_recv,
        device_id=sibling,
    )
    cross.start()
    first_core = kv == 0
    mine = jnp.where(first_core, terms[:half], terms[half:])
    residual = jnp.where(first_core, tokf[:half], tokf[half:])
    cross.wait_recv()
    middle = (residual + (mine + head_in[...])).astype(BF).astype(F32)
    normed_two = rms_scaled(middle, gains[1:2, :])

    l_wr.wait()
    topk = routes_s.shape[0]
    lane = lax.broadcasted_iota(jnp.int32, (half, 128), 1)
    row = lax.broadcasted_iota(jnp.int32, (half, 128), 0)

    route = []
    for j in range(topk):
        named_by = jnp.zeros((half, 128), jnp.int32)
        for i in range(half):
            named_by = jnp.where(row == i, routes_s[j, i], named_by)
        route.append(named_by)

    def places(expert, slot):
        named = jnp.zeros((half, 128), F32)
        for j in range(topk):
            named = named + jnp.where(route[j] == expert, 1.0, 0.0)
        rank = jnp.zeros((half, 128), F32)
        for i in range(half - 1):
            rank = rank + jnp.where(row > i, named[i : i + 1, :], 0.0)
        return jnp.where(rank == slot.astype(F32), named, 0.0)

    pick = places(lane % experts, lane // experts)
    pick_t = jnp.transpose(pick)[: 2 * experts, :].astype(BF)
    outgoing = jnp.dot(pick_t, normed_two, preferred_element_type=F32)
    for c in range(cols):
        for k in range(2):
            wide_a[pl.ds(c * 2 + k, experts, stride=2 * cols), :] = outgoing[
                k * experts : (k + 1) * experts, c * hd : (c + 1) * hd
            ]
    disp_out[...] = wide_a[...].reshape(experts, 2 * cols, hd).astype(BF)
    to_all(lambda peer: disp_out.at[peer // 2], disp_in, 2)

    logits = lax.dot_general(normed_two, wr[...], LAST, preferred_element_type=F32)
    choice = lax.broadcasted_iota(jnp.int32, logits.shape, 1)
    chosen = [
        jnp.sum(jnp.where(choice == route[j][:, :experts], logits, 0.0), axis=-1, keepdims=True)
        for j in range(topk)
    ]
    best = functools.reduce(jnp.maximum, chosen)
    powers = [jnp.exp(c - best) for c in chosen]
    denom = functools.reduce(jnp.add, powers)
    peer_expert = (lane % n) // 2
    blend = jnp.zeros((half, 128), F32)
    for j in range(topk):
        blend = blend + jnp.where(route[j] == peer_expert, powers[j] / denom, 0.0)
    blend = blend * places(peer_expert, lane // n)
    part_a = blend.astype(BF).astype(F32)
    part_b = (blend - part_a).astype(BF).astype(F32)
    part_c = blend - part_a - part_b
    blend_parts = jnp.concatenate([part_a, part_b, part_c], axis=0).astype(BF)

    l_wg.wait()
    l_wu.wait()
    l_wd.wait()
    for swap in swaps:
        swap.wait_recv()
    wait_bytes(disp_in, recv_sems.at[2])
    wide_b[...] = disp_in[...].astype(F32).reshape(n * 2 * cols, hd)

    def unpack():
        return jnp.concatenate(
            [
                jnp.concatenate(
                    [
                        wide_b[pl.ds(c * 2 + k, n, stride=2 * cols), :].astype(BF)
                        for c in range(cols)
                    ],
                    axis=1,
                )
                for k in range(2)
            ],
            axis=0,
        )

    arrived = unpack()
    result = None
    for t in range(2):
        gate = lax.dot_general(arrived, wg[t], LAST, preferred_element_type=F32)
        up = lax.dot_general(arrived, wu[t], LAST, preferred_element_type=F32)
        hidden = (jnp.maximum(gate, 0.0) * up).astype(BF)
        part = jnp.dot(hidden, wd[t], preferred_element_type=F32)
        result = part if result is None else result + part
    for c in range(cols):
        for k in range(2):
            wide_b[pl.ds(c * 2 + k, n, stride=2 * cols), :] = result[
                k * n : (k + 1) * n, c * hd : (c + 1) * hd
            ]
    ret_out[...] = wide_b[...].reshape(n, 2 * cols, hd).astype(BF)
    to_all(lambda peer: ret_out.at[peer], ret_in, 3)
    wait_bytes(ret_in, recv_sems.at[3])
    wide_b[...] = ret_in[...].astype(F32).reshape(n * 2 * cols, hd)
    mixed = jnp.dot(blend_parts, unpack(), preferred_element_type=F32)
    mixed = mixed[:half] + mixed[half : 2 * half] + mixed[2 * half :]
    out_ref[...] = (middle + mixed).astype(BF)

    cross.wait_send()
    for swap in swaps:
        swap.wait_send()
    for phase, ref in enumerate((q_in, a_in, disp_in, ret_in)):
        wait_bytes(ref.at[pl.ds(0, n - 1)], send_sems.at[phase])


def solution(mesh):
    n = mesh.shape["req"]

    def shards(
        tokens,
        gain_attn,
        w_query,
        w_key,
        w_value,
        w_out,
        cache_k,
        cache_v,
        page_table,
        lengths,
        new_owner,
        gain_moe,
        w_router,
        routes,
        w_gate,
        w_up,
        w_down,
    ):
        slots, width = tokens.shape
        half = slots // 2
        hd = w_key.shape[1]
        cols = width // hd
        experts = n // 2
        span = page_table.shape[1] * cache_k.shape[1]
        gains = jnp.stack([gain_attn, gain_moe]).astype(F32)
        hidden = w_gate.shape[2]
        smem = pl.BlockSpec(memory_space=pltpu.SMEM)
        hbm = pl.BlockSpec(memory_space=pl.ANY)
        dma = pltpu.SemaphoreType.DMA
        return pl.pallas_call(
            functools.partial(layer_kernel, n),
            out_shape=jax.ShapeDtypeStruct((half, width), BF),
            in_specs=[smem] * 4 + [hbm] * 12,
            out_specs=pl.BlockSpec(memory_space=pltpu.VMEM),
            scratch_shapes=[
                pltpu.VMEM((slots, width), BF),
                pltpu.VMEM((2, width), F32),
                pltpu.VMEM((width, w_query.shape[1] + 2 * hd), BF),
                pltpu.VMEM(w_out.shape, BF),
                pltpu.VMEM(cache_k.shape, BF),
                pltpu.VMEM(cache_v.shape, BF),
                pltpu.VMEM(w_router.shape[::-1], BF),
                pltpu.VMEM((2, hidden, width), BF),
                pltpu.VMEM((2, hidden, width), BF),
                pltpu.VMEM((2, hidden, width), BF),
                pltpu.VMEM((slots * 8, hd), F32),
                pltpu.VMEM((slots * 8, span), F32),
                pltpu.VMEM((slots * 8, hd), F32),
                pltpu.VMEM((8, hd), BF),
                pltpu.VMEM((n, 8, hd), BF),
                pltpu.VMEM((8, hd), BF),
                pltpu.VMEM((n, 8, hd), BF),
                pltpu.VMEM((2, half, width), F32),
                pltpu.VMEM((half, width), F32),
                pltpu.VMEM((experts * 2 * cols, hd), F32),
                pltpu.VMEM((experts, 2 * cols, hd), BF),
                pltpu.VMEM((n, 2 * cols, hd), BF),
                pltpu.VMEM((n * 2 * cols, hd), F32),
                pltpu.VMEM((n, 2 * cols, hd), BF),
                pltpu.VMEM((n, 2 * cols, hd), BF),
                dma((12,)),
                dma((3,)),
                dma((3,)),
                dma,
                dma,
                dma((4,)),
                dma((4,)),
            ],
            compiler_params=pltpu.CompilerParams(
                collective_id=0, has_side_effects=True, vmem_limit_bytes=60 * 1024 * 1024
            ),
        )(
            page_table.T,
            lengths,
            new_owner,
            routes.T,
            tokens,
            gains,
            w_query,
            w_key,
            w_value,
            w_out,
            cache_k,
            cache_v,
            w_router.T,
            jnp.swapaxes(w_gate, 1, 2),
            jnp.swapaxes(w_up, 1, 2),
            jnp.swapaxes(w_down, 1, 2),
        )

    return jax.shard_map(
        shards,
        mesh=mesh,
        in_specs=(
            P("req", None),
            P(),
            P(None, "kv"),
            P(None, "kv"),
            P(None, "kv"),
            P("kv", None),
            P("req", None, "kv"),
            P("req", None, "kv"),
            P("req", None),
            P(),
            P(),
            P(),
            P(),
            P(("req", "kv"), None),
            P("req", None, "kv"),
            P("req", None, "kv"),
            P("req", None, "kv"),
        ),
        out_specs=P(("req", "kv"), None),
        check_vma=False,
    )
```

```python
import functools

import jax
import jax.numpy as jnp
from jax import lax
from jax.experimental import pallas as pl
from jax.experimental.pallas import tpu as pltpu
from jax.sharding import PartitionSpec as P

BF = jnp.bfloat16
F32 = jnp.float32
LAST = (((1,), (1,)), ((), ()))


def rms_scaled(wide, gain_row):
    squares = jnp.mean(wide * wide, axis=-1, keepdims=True)
    return (wide * lax.rsqrt(squares + 1e-06) * gain_row).astype(BF)


def wait_bytes(ref, sem):
    pltpu.make_async_copy(ref, ref, sem).wait()


def layer_kernel(
    n,
    pages_s,
    lengths_s,
    owner_s,
    routes_s,
    tokens_h,
    gains_h,
    wq_h,
    wk_h,
    wv_h,
    wo_h,
    ck_h,
    cv_h,
    wr_h,
    wg_h,
    wu_h,
    wd_h,
    out_ref,
    tok,
    gains,
    wqkv,
    wo,
    ck,
    cv,
    wr,
    wg,
    wu,
    wd,
    heads,
    scores,
    att,
    q_out,
    q_in,
    head_sum,
    head_in,
    wide_a,
    disp_out,
    disp_in,
    wide_b,
    ret_out,
    ret_in,
    fin,
    row_sum,
    row_in,
    t_out,
    t_in,
    m_wide,
    m_out,
    m_in,
    wide_m,
    late_out,
    late_in,
    load_sems,
    w_send,
    w_recv,
    h_send,
    h_recv,
    r_send,
    r_recv,
    send_sems,
    recv_sems,
    line_x,
    line_z,
):
    me = lax.axis_index("req")
    kv = lax.axis_index("kv")
    slots, width = tok.shape
    half = slots // 2
    hd = ck.shape[2]
    page = ck.shape[1]
    per_slot = pages_s.shape[0]
    groups = wo.shape[0] // hd
    experts = n // 2
    cols = width // hd
    inv_root = hd ** (-0.5)

    def load(src, dst, i):
        copy = pltpu.make_async_copy(src, dst, load_sems.at[i])
        copy.start()
        return copy

    qcols = wq_h.shape[1]
    l_tok = load(tokens_h, tok, 0)
    l_gain = load(gains_h, gains, 1)
    l_wq = load(wq_h, wqkv.at[:, pl.ds(0, qcols)], 2)
    l_wk = load(wk_h, wqkv.at[:, pl.ds(qcols, hd)], 3)
    l_wv = load(wv_h, wqkv.at[:, pl.ds(qcols + hd, hd)], 4)
    l_ck = load(ck_h, ck, 5)
    l_cv = load(cv_h, cv, 6)
    l_wo = load(wo_h, wo, 7)
    l_wr = load(wr_h, wr, 8)
    l_wg = load(wg_h.at[0], wg.at[0], 9)
    l_wu = load(wu_h.at[0], wu.at[0], 10)
    l_wd = load(wd_h.at[0], wd.at[0], 11)

    def line(stride, i):
        spot = lax.rem(me // stride, 4)
        return {"req": me + (lax.rem(spot + i, 4) - spot) * stride}

    def greet(sem, stride):
        for i in range(1, 4):
            pl.semaphore_signal(sem, 1, device_id=line(stride, i))

    sibling = {"kv": 1 - kv}
    relocating = kv == 1
    barrier = pltpu.get_barrier_semaphore()
    pl.semaphore_signal(barrier, 1, device_id=sibling)
    for stride in (1, 4, 16):
        greet(barrier, stride)

    def to_all(src_of, dst, phase):
        def send(i, carry):
            peer = lax.rem(me + i, n)
            pltpu.make_async_remote_copy(
                src_ref=src_of(peer),
                dst_ref=dst.at[me],
                send_sem=send_sems.at[phase],
                recv_sem=recv_sems.at[phase],
                device_id={"req": peer},
            ).start()
            return carry

        pltpu.make_async_copy(src_of(me), dst.at[me], recv_sems.at[phase]).start()
        lax.fori_loop(1, n, send, 0)

    l_tok.wait()
    l_gain.wait()
    tokf = tok[...].astype(F32)
    normed = rms_scaled(tokf, gains[0:1, :])
    last = (slots - 1) * 8
    m_wide[...] = jnp.zeros((16, hd), F32)
    for c in range(cols):
        m_wide[c : c + 1, :] = tokf[slots - 1 : slots, c * hd : (c + 1) * hd]
    t_out[...] = m_wide[...].astype(BF)
    pl.semaphore_wait(barrier, 10)
    greet(line_x, 4)
    swaps = []
    for i, (src, dst) in enumerate(((wg_h, wg), (wu_h, wu), (wd_h, wd))):
        swap = pltpu.make_async_remote_copy(
            src_ref=src.at[0],
            dst_ref=dst.at[1],
            send_sem=w_send.at[i],
            recv_sem=w_recv.at[i],
            device_id=sibling,
        )
        swap.start()
        swaps.append(swap)
    pl.semaphore_wait(line_x, 3)
    greet(line_z, 16)
    l_wq.wait()
    l_wk.wait()
    l_wv.wait()
    qkv = jnp.dot(normed, wqkv[...], preferred_element_type=F32).astype(BF).astype(F32)
    for h in range(groups + 2):
        heads[pl.ds(h, slots, stride=8), :] = qkv[:, h * hd : (h + 1) * hd]
    q_out[...] = heads[last : last + 8, :].astype(BF)
    pl.semaphore_wait(line_z, 3)
    to_all(lambda peer: q_out, q_in, 0)

    @pl.when(relocating)
    def _():
        to_all(lambda peer: t_out, t_in, 1)

    def attend(first, count):
        rows = slice(first * 8, (first + count) * 8)
        place = lax.broadcasted_iota(jnp.int32, (8, page), 1)
        for s in range(first, first + count):
            block = heads[s * 8 : s * 8 + 8, :].astype(BF)
            live = lengths_s[me * slots + s]
            for j in range(per_slot):
                dots = lax.dot_general(
                    block, ck[pages_s[j, s]], LAST, preferred_element_type=F32
                )
                scores[s * 8 : s * 8 + 8, j * page : (j + 1) * page] = jnp.where(
                    place + j * page < live, dots * inv_root, -1e30
                )
        all_scores = scores[rows, :]
        top = jnp.max(all_scores, axis=-1, keepdims=True)
        weights = jnp.exp(all_scores - top)
        total = jnp.sum(weights, axis=-1, keepdims=True)
        scores[rows, :] = weights
        for s in range(first, first + count):
            acc = jnp.zeros((8, hd), F32)
            for j in range(per_slot):
                acc = acc + jnp.dot(
                    scores[s * 8 : s * 8 + 8, j * page : (j + 1) * page].astype(BF),
                    cv[pages_s[j, s]],
                    preferred_element_type=F32,
                )
            att[s * 8 : s * 8 + 8, :] = acc
        block = heads[rows, :].reshape(count, 8, hd)
        own = jnp.sum(block * block[:, groups : groups + 1, :], axis=-1, keepdims=True) * inv_root
        top = top.reshape(count, 8, 1)
        total = total.reshape(count, 8, 1)
        joint = jnp.maximum(top, own)
        old_part = jnp.exp(top - joint)
        new_part = jnp.exp(own - joint)
        merged = (
            att[rows, :].reshape(count, 8, hd) * old_part
            + new_part * block[:, groups + 1 : groups + 2, :]
        )
        result = merged / (total * old_part + new_part)
        att[rows, :] = result.astype(BF).astype(F32).reshape(count * 8, hd)

    l_ck.wait()
    l_cv.wait()
    attend(0, slots - 1)
    att[last : last + 8, :] = jnp.zeros((8, hd), F32)
    l_wo.wait()

    def head_terms():
        attended = jnp.concatenate(
            [att[pl.ds(h, slots, stride=8), :].astype(BF) for h in range(groups)], axis=1
        )
        return jnp.dot(attended, wo[...], preferred_element_type=F32)

    terms = head_terms()
    head_sum[0] = terms[:half]
    head_sum[1] = terms[half:]
    cross = pltpu.make_async_remote_copy(
        src_ref=head_sum.at[1 - kv],
        dst_ref=head_in,
        send_sem=h_send,
        recv_sem=h_recv,
        device_id=sibling,
    )
    cross.start()
    first_core = kv == 0
    mine = jnp.where(first_core, terms[:half], terms[half:])
    residual = jnp.where(first_core, tokf[:half], tokf[half:])

    topk = routes_s.shape[0]
    lane = lax.broadcasted_iota(jnp.int32, (half, 128), 1)
    row = lax.broadcasted_iota(jnp.int32, (half, 128), 0)
    late_row = (row == half - 1) & relocating
    route = []
    for j in range(topk):
        named_by = jnp.zeros((half, 128), jnp.int32)
        for i in range(half):
            named_by = jnp.where(row == i, routes_s[j, i], named_by)
        route.append(named_by)
    early = [jnp.where(late_row, -1, r) for r in route]

    def places(expert, slot):
        named = jnp.zeros((half, 128), F32)
        for j in range(topk):
            named = named + jnp.where(early[j] == expert, 1.0, 0.0)
        rank = jnp.zeros((half, 128), F32)
        for i in range(half - 1):
            rank = rank + jnp.where(row > i, named[i : i + 1, :], 0.0)
        return jnp.where(rank == slot.astype(F32), named, 0.0)

    pick = places(lane % experts, lane // experts)
    pick_t = jnp.transpose(pick)[: 2 * experts, :].astype(BF)
    peer_expert = (lane % n) // 2
    peer_place = places(peer_expert, lane // n)

    cross.wait_recv()
    middle = (residual + (mine + head_in[...])).astype(BF).astype(F32)
    normed_two = rms_scaled(middle, gains[1:2, :])
    outgoing = jnp.dot(pick_t, normed_two, preferred_element_type=F32)
    for c in range(cols):
        for k in range(2):
            wide_a[pl.ds(c * 2 + k, experts, stride=2 * cols), :] = outgoing[
                k * experts : (k + 1) * experts, c * hd : (c + 1) * hd
            ]
    disp_out[...] = wide_a[...].reshape(experts, 2 * cols, hd).astype(BF)
    to_all(lambda peer: disp_out.at[peer // 2], disp_in, 2)

    wait_bytes(q_in, recv_sems.at[0])
    served = owner_s[me]
    heads[last : last + 8, :] = q_in[served].astype(F32)
    attend(slots - 1, 1)
    late_terms = head_terms()[slots - 1 : slots, :]
    row_sum[...] = late_terms

    def row_copy():
        return pltpu.make_async_remote_copy(
            src_ref=row_sum,
            dst_ref=row_in,
            send_sem=r_send,
            recv_sem=r_recv,
            device_id=sibling,
        )

    @pl.when(first_core)
    def _():
        row_copy().start()

    l_wr.wait()

    def route_weights(normed_rows, chosen_by):
        logits = lax.dot_general(normed_rows, wr[...], LAST, preferred_element_type=F32)
        choice = lax.broadcasted_iota(jnp.int32, logits.shape, 1)
        chosen = [
            jnp.sum(jnp.where(choice == r[:, :experts], logits, 0.0), axis=-1, keepdims=True)
            for r in chosen_by
        ]
        best = functools.reduce(jnp.maximum, chosen)
        powers = [jnp.exp(c - best) for c in chosen]
        denom = functools.reduce(jnp.add, powers)
        blend = jnp.zeros((half, 128), F32)
        for r, power in zip(chosen_by, powers):
            blend = blend + jnp.where(r == peer_expert, power / denom, 0.0)
        return blend

    def in_parts(blend):
        part_a = blend.astype(BF).astype(F32)
        part_b = (blend - part_a).astype(BF).astype(F32)
        part_c = blend - part_a - part_b
        return jnp.concatenate([part_a, part_b, part_c], axis=0).astype(BF)

    def blended(parts, rows):
        mixed = jnp.dot(parts, rows, preferred_element_type=F32)
        return mixed[:half] + mixed[half : 2 * half] + mixed[2 * half :]

    blend_parts = in_parts(route_weights(normed_two, early) * peer_place)

    @pl.when(relocating)
    def _():
        wait_bytes(t_in, recv_sems.at[1])
        row_copy().wait_recv()
        total = row_sum[...] + row_in[...]
        for c in range(cols):
            m_wide[c : c + 1, :] = total[:, c * hd : (c + 1) * hd]
        m_out[...] = (t_in[served].astype(F32) + m_wide[...]).astype(BF)
        to_all(lambda peer: m_out, m_in, 3)

    def run_expert(rows):
        result = None
        for t in range(2):
            gate = lax.dot_general(rows, wg[t], LAST, preferred_element_type=F32)
            up = lax.dot_general(rows, wu[t], LAST, preferred_element_type=F32)
            hidden = (jnp.maximum(gate, 0.0) * up).astype(BF)
            part = jnp.dot(hidden, wd[t], preferred_element_type=F32)
            result = part if result is None else result + part
        return result

    def unpack(wide, first, stride):
        return jnp.concatenate(
            [wide[pl.ds(first(c), n, stride=stride), :] for c in range(cols)], axis=1
        )

    def unpack_pair():
        return jnp.concatenate(
            [unpack(wide_b, lambda c: c * 2 + k, 2 * cols).astype(BF) for k in range(2)], axis=0
        )

    l_wg.wait()
    l_wu.wait()
    l_wd.wait()
    for swap in swaps:
        swap.wait_recv()
    wait_bytes(disp_in, recv_sems.at[2])
    wide_b[...] = disp_in[...].astype(F32).reshape(n * 2 * cols, hd)
    result = run_expert(unpack_pair())
    for c in range(cols):
        for k in range(2):
            wide_b[pl.ds(c * 2 + k, n, stride=2 * cols), :] = result[
                k * n : (k + 1) * n, c * hd : (c + 1) * hd
            ]
    ret_out[...] = wide_b[...].reshape(n, 2 * cols, hd).astype(BF)
    to_all(lambda peer: ret_out.at[peer], ret_in, 4)

    @pl.when(relocating)
    def _():
        owners = jnp.zeros((8, 128), jnp.int32)
        owner_lane = lax.broadcasted_iota(jnp.int32, (8, 128), 1)
        for c in range(n):
            owners = jnp.where(owner_lane == c, owner_s[c], owners)
        slot_row = lax.broadcasted_iota(jnp.int32, (n, n), 0)
        moves = jnp.where(slot_row == owners[0:1, :n], 1.0, 0.0).astype(BF)
        wait_bytes(m_in, recv_sems.at[3])
        wide_m[...] = m_in[...].astype(F32).reshape(n * 16, hd)
        late_normed = rms_scaled(unpack(wide_m, lambda c: c, 16), gains[1:2, :])
        ordered = jnp.dot(moves, late_normed, preferred_element_type=F32).astype(BF)
        late_result = run_expert(ordered)

        def find(c, found):
            return jnp.where(owner_s[c] == me, c, found)

        origin = lax.fori_loop(0, n, find, 0)
        late_middle = jnp.concatenate(
            [wide_m[pl.ds(origin * 16 + c, 1), :] for c in range(cols)], axis=1
        )
        late_middle = jnp.broadcast_to(late_middle, (half, width))
        late_blend = in_parts(
            jnp.where(
                lane < n,
                route_weights(rms_scaled(late_middle, gains[1:2, :]), route),
                0.0,
            )[:, :n]
        )
        for c in range(cols):
            wide_m[pl.ds(c, n, stride=16), :] = late_result[:, c * hd : (c + 1) * hd]
        late_out[...] = wide_m[...].reshape(n, 16, hd).astype(BF)
        to_all(lambda peer: late_out.at[peer], late_in, 5)
        wait_bytes(late_in, recv_sems.at[5])
        wide_m[...] = late_in[...].astype(F32).reshape(n * 16, hd)
        late = late_middle + blended(late_blend, unpack(wide_m, lambda c: c, 16).astype(BF))
        fin[half - 1 : half, :] = late[half - 1 : half, :]

    wait_bytes(ret_in, recv_sems.at[4])
    wide_b[...] = ret_in[...].astype(F32).reshape(n * 2 * cols, hd)
    done = middle + blended(blend_parts, unpack_pair())
    kept = (lax.broadcasted_iota(jnp.int32, (half, width), 0) == half - 1) & relocating
    out_ref[...] = jnp.where(kept, fin[...], done).astype(BF)

    cross.wait_send()
    for swap in swaps:
        swap.wait_send()
    for phase, ref in ((0, q_in), (2, disp_in), (4, ret_in)):
        wait_bytes(ref.at[pl.ds(0, n - 1)], send_sems.at[phase])

    @pl.when(first_core)
    def _():
        row_copy().wait_send()

    @pl.when(relocating)
    def _():
        for phase, ref in ((1, t_in), (3, m_in), (5, late_in)):
            wait_bytes(ref.at[pl.ds(0, n - 1)], send_sems.at[phase])


def solution(mesh):
    n = mesh.shape["req"]

    def shards(
        tokens,
        gain_attn,
        w_query,
        w_key,
        w_value,
        w_out,
        cache_k,
        cache_v,
        page_table,
        lengths,
        new_owner,
        gain_moe,
        w_router,
        routes,
        w_gate,
        w_up,
        w_down,
    ):
        slots, width = tokens.shape
        half = slots // 2
        hd = w_key.shape[1]
        cols = width // hd
        experts = n // 2
        span = page_table.shape[1] * cache_k.shape[1]
        gains = jnp.stack([gain_attn, gain_moe]).astype(F32)
        hidden = w_gate.shape[2]
        smem = pl.BlockSpec(memory_space=pltpu.SMEM)
        hbm = pl.BlockSpec(memory_space=pl.ANY)
        dma = pltpu.SemaphoreType.DMA
        return pl.pallas_call(
            functools.partial(layer_kernel, n),
            out_shape=jax.ShapeDtypeStruct((half, width), BF),
            in_specs=[smem] * 4 + [hbm] * 12,
            out_specs=pl.BlockSpec(memory_space=pltpu.VMEM),
            scratch_shapes=[
                pltpu.VMEM((slots, width), BF),
                pltpu.VMEM((2, width), F32),
                pltpu.VMEM((width, w_query.shape[1] + 2 * hd), BF),
                pltpu.VMEM(w_out.shape, BF),
                pltpu.VMEM(cache_k.shape, BF),
                pltpu.VMEM(cache_v.shape, BF),
                pltpu.VMEM(w_router.shape[::-1], BF),
                pltpu.VMEM((2, hidden, width), BF),
                pltpu.VMEM((2, hidden, width), BF),
                pltpu.VMEM((2, hidden, width), BF),
                pltpu.VMEM((slots * 8, hd), F32),
                pltpu.VMEM((slots * 8, span), F32),
                pltpu.VMEM((slots * 8, hd), F32),
                pltpu.VMEM((8, hd), BF),
                pltpu.VMEM((n, 8, hd), BF),
                pltpu.VMEM((2, half, width), F32),
                pltpu.VMEM((half, width), F32),
                pltpu.VMEM((experts * 2 * cols, hd), F32),
                pltpu.VMEM((experts, 2 * cols, hd), BF),
                pltpu.VMEM((n, 2 * cols, hd), BF),
                pltpu.VMEM((n * 2 * cols, hd), F32),
                pltpu.VMEM((n, 2 * cols, hd), BF),
                pltpu.VMEM((n, 2 * cols, hd), BF),
                pltpu.VMEM((half, width), F32),
                pltpu.VMEM((1, width), F32),
                pltpu.VMEM((1, width), F32),
                pltpu.VMEM((16, hd), BF),
                pltpu.VMEM((n, 16, hd), BF),
                pltpu.VMEM((16, hd), F32),
                pltpu.VMEM((16, hd), BF),
                pltpu.VMEM((n, 16, hd), BF),
                pltpu.VMEM((n * 16, hd), F32),
                pltpu.VMEM((n, 16, hd), BF),
                pltpu.VMEM((n, 16, hd), BF),
                dma((12,)),
                dma((3,)),
                dma((3,)),
                dma,
                dma,
                dma,
                dma,
                dma((6,)),
                dma((6,)),
                pltpu.SemaphoreType.REGULAR,
                pltpu.SemaphoreType.REGULAR,
            ],
            compiler_params=pltpu.CompilerParams(
                collective_id=0, has_side_effects=True, vmem_limit_bytes=60 * 1024 * 1024
            ),
        )(
            page_table.T,
            lengths,
            new_owner,
            routes.T,
            tokens,
            gains,
            w_query,
            w_key,
            w_value,
            w_out,
            cache_k,
            cache_v,
            w_router.T,
            jnp.swapaxes(w_gate, 1, 2),
            jnp.swapaxes(w_up, 1, 2),
            jnp.swapaxes(w_down, 1, 2),
        )

    return jax.shard_map(
        shards,
        mesh=mesh,
        in_specs=(
            P("req", None),
            P(),
            P(None, "kv"),
            P(None, "kv"),
            P(None, "kv"),
            P("kv", None),
            P("req", None, "kv"),
            P("req", None, "kv"),
            P("req", None),
            P(),
            P(),
            P(),
            P(),
            P(("req", "kv"), None),
            P("req", None, "kv"),
            P("req", None, "kv"),
            P("req", None, "kv"),
        ),
        out_specs=P(("req", "kv"), None),
        check_vma=False,
    )
```

```python
import functools

import jax
import jax.numpy as jnp
from jax import lax
from jax.experimental import pallas as pl
from jax.experimental.pallas import tpu as pltpu
from jax.sharding import PartitionSpec as P

BF = jnp.bfloat16
F32 = jnp.float32
LAST = (((1,), (1,)), ((), ()))


def rms_scaled(wide, gain_row):
    squares = jnp.mean(wide * wide, axis=-1, keepdims=True)
    return (wide * lax.rsqrt(squares + 1e-06) * gain_row).astype(BF)


def wait_bytes(ref, sem):
    pltpu.make_async_copy(ref, ref, sem).wait()


def layer_kernel(
    n,
    pages_h,
    lengths_h,
    owner_h,
    routes_h,
    tokens_h,
    gain_a_h,
    gain_m_h,
    wq_h,
    wk_h,
    wv_h,
    wo_h,
    ck_h,
    cv_h,
    wr_h,
    wg_h,
    wu_h,
    wd_h,
    out_ref,
    tok,
    gain_a,
    gain_m,
    wqkv,
    wo,
    ck,
    cv,
    wr,
    wg,
    wu,
    wd,
    heads,
    scores,
    att,
    q_out,
    q_in,
    head_sum,
    head_in,
    wide_a,
    disp_out,
    disp_in,
    wide_b,
    ret_out,
    ret_in,
    pages_s,
    lengths_s,
    owner_s,
    routes_s,
    fin,
    row_sum,
    row_in,
    t_out,
    t_in,
    m_wide,
    m_out,
    m_in,
    wide_m,
    late_out,
    late_in,
    load_sems,
    w_send,
    w_recv,
    h_send,
    h_recv,
    r_send,
    r_recv,
    send_sems,
    recv_sems,
):
    me = lax.axis_index("req")
    kv = lax.axis_index("kv")
    slots, width = tok.shape
    half = slots // 2
    hd = ck.shape[2]
    page = ck.shape[1]
    per_slot = pages_s.shape[0]
    groups = wo.shape[0] // hd
    experts = n // 2
    cols = width // hd
    inv_root = hd ** (-0.5)

    def load(src, dst, i):
        copy = pltpu.make_async_copy(src, dst, load_sems.at[i])
        copy.start()
        return copy

    qcols = wq_h.shape[1]
    l_tok = load(tokens_h, tok, 0)
    l_gain = load(gain_a_h, gain_a, 1)
    l_gain_m = load(gain_m_h, gain_m, 12)
    l_wq = load(wq_h, wqkv.at[:, pl.ds(0, qcols)], 2)
    l_wk = load(wk_h, wqkv.at[:, pl.ds(qcols, hd)], 3)
    l_wv = load(wv_h, wqkv.at[:, pl.ds(qcols + hd, hd)], 4)

    sibling = {"kv": 1 - kv}
    relocating = kv == 1
    barrier = pltpu.get_barrier_semaphore()

    def greet(i, carry):
        pl.semaphore_signal(barrier, 1, device_id={"req": lax.rem(me + i, n)})
        return carry

    pl.semaphore_signal(barrier, 1, device_id=sibling)
    lax.fori_loop(1, n, greet, 0)
    l_ints = [
        load(src, dst, 13 + i)
        for i, (src, dst) in enumerate(
            (
                (pages_h, pages_s),
                (lengths_h, lengths_s),
                (owner_h, owner_s),
                (routes_h, routes_s),
            )
        )
    ]
    l_ck = load(ck_h, ck, 5)
    l_cv = load(cv_h, cv, 6)
    l_wo = load(wo_h, wo, 7)
    l_wr = load(wr_h, wr, 8)
    l_wg = load(wg_h.at[0], wg.at[0], 9)
    l_wu = load(wu_h.at[0], wu.at[0], 10)
    l_wd = load(wd_h.at[0], wd.at[0], 11)

    def to_all(src_of, dst, phase):
        def send(i, carry):
            peer = lax.rem(me + i, n)
            pltpu.make_async_remote_copy(
                src_ref=src_of(peer),
                dst_ref=dst.at[me],
                send_sem=send_sems.at[phase],
                recv_sem=recv_sems.at[phase],
                device_id={"req": peer},
            ).start()
            return carry

        pltpu.make_async_copy(src_of(me), dst.at[me], recv_sems.at[phase]).start()
        lax.fori_loop(1, n, send, 0)

    l_tok.wait()
    l_gain.wait()
    l_gain_m.wait()
    gain_attn = gain_a[...].astype(F32).reshape(1, width)
    gain_moe = gain_m[...].astype(F32).reshape(1, width)
    tokf = tok[...].astype(F32)
    normed = rms_scaled(tokf, gain_attn)
    last = (slots - 1) * 8
    m_wide[...] = jnp.zeros((16, hd), F32)
    for c in range(cols):
        m_wide[c : c + 1, :] = tokf[slots - 1 : slots, c * hd : (c + 1) * hd]
    t_out[...] = m_wide[...].astype(BF)
    l_wq.wait()
    l_wk.wait()
    l_wv.wait()
    qkv = jnp.dot(normed, wqkv[...], preferred_element_type=F32).astype(BF).astype(F32)
    for h in range(groups + 2):
        heads[pl.ds(h, slots, stride=8), :] = qkv[:, h * hd : (h + 1) * hd]
    q_out[...] = heads[last : last + 8, :].astype(BF)
    pl.semaphore_wait(barrier, n)
    to_all(lambda peer: q_out, q_in, 0)

    @pl.when(relocating)
    def _():
        to_all(lambda peer: t_out, t_in, 1)

    swaps = []
    for i, (src, dst) in enumerate(((wg_h, wg), (wu_h, wu), (wd_h, wd))):
        swap = pltpu.make_async_remote_copy(
            src_ref=src.at[0],
            dst_ref=dst.at[1],
            send_sem=w_send.at[i],
            recv_sem=w_recv.at[i],
            device_id=sibling,
        )
        swap.start()
        swaps.append(swap)

    def attend(first, count):
        rows = slice(first * 8, (first + count) * 8)
        place = lax.broadcasted_iota(jnp.int32, (8, page), 1)
        for s in range(first, first + count):
            block = heads[s * 8 : s * 8 + 8, :].astype(BF)
            live = lengths_s[me * slots + s]
            for j in range(per_slot):
                dots = lax.dot_general(
                    block, ck[pages_s[j, s]], LAST, preferred_element_type=F32
                )
                scores[s * 8 : s * 8 + 8, j * page : (j + 1) * page] = jnp.where(
                    place + j * page < live, dots * inv_root, -1e30
                )
        all_scores = scores[rows, :]
        top = jnp.max(all_scores, axis=-1, keepdims=True)
        weights = jnp.exp(all_scores - top)
        total = jnp.sum(weights, axis=-1, keepdims=True)
        scores[rows, :] = weights
        for s in range(first, first + count):
            acc = jnp.zeros((8, hd), F32)
            for j in range(per_slot):
                acc = acc + jnp.dot(
                    scores[s * 8 : s * 8 + 8, j * page : (j + 1) * page].astype(BF),
                    cv[pages_s[j, s]],
                    preferred_element_type=F32,
                )
            att[s * 8 : s * 8 + 8, :] = acc
        block = heads[rows, :].reshape(count, 8, hd)
        own = jnp.sum(block * block[:, groups : groups + 1, :], axis=-1, keepdims=True) * inv_root
        top = top.reshape(count, 8, 1)
        total = total.reshape(count, 8, 1)
        joint = jnp.maximum(top, own)
        old_part = jnp.exp(top - joint)
        new_part = jnp.exp(own - joint)
        merged = (
            att[rows, :].reshape(count, 8, hd) * old_part
            + new_part * block[:, groups + 1 : groups + 2, :]
        )
        result = merged / (total * old_part + new_part)
        att[rows, :] = result.astype(BF).astype(F32).reshape(count * 8, hd)

    for l_int in l_ints:
        l_int.wait()
    l_ck.wait()
    l_cv.wait()
    attend(0, slots - 1)
    att[last : last + 8, :] = jnp.zeros((8, hd), F32)
    l_wo.wait()

    def head_terms():
        attended = jnp.concatenate(
            [att[pl.ds(h, slots, stride=8), :].astype(BF) for h in range(groups)], axis=1
        )
        return jnp.dot(attended, wo[...], preferred_element_type=F32)

    terms = head_terms()
    head_sum[0] = terms[:half]
    head_sum[1] = terms[half:]
    cross = pltpu.make_async_remote_copy(
        src_ref=head_sum.at[1 - kv],
        dst_ref=head_in,
        send_sem=h_send,
        recv_sem=h_recv,
        device_id=sibling,
    )
    cross.start()
    first_core = kv == 0
    mine = jnp.where(first_core, terms[:half], terms[half:])
    residual = jnp.where(first_core, tokf[:half], tokf[half:])

    topk = routes_s.shape[0]
    lane = lax.broadcasted_iota(jnp.int32, (half, 128), 1)
    row = lax.broadcasted_iota(jnp.int32, (half, 128), 0)
    late_row = (row == half - 1) & relocating
    route = []
    for j in range(topk):
        named_by = jnp.zeros((half, 128), jnp.int32)
        for i in range(half):
            named_by = jnp.where(row == i, routes_s[j, i], named_by)
        route.append(named_by)
    early = [jnp.where(late_row, -1, r) for r in route]

    def places(expert, slot):
        named = jnp.zeros((half, 128), F32)
        for j in range(topk):
            named = named + jnp.where(early[j] == expert, 1.0, 0.0)
        rank = jnp.zeros((half, 128), F32)
        for i in range(half - 1):
            rank = rank + jnp.where(row > i, named[i : i + 1, :], 0.0)
        return jnp.where(rank == slot.astype(F32), named, 0.0)

    pick = places(lane % experts, lane // experts)
    pick_t = jnp.transpose(pick)[: 2 * experts, :].astype(BF)
    peer_expert = (lane % n) // 2
    peer_place = places(peer_expert, lane // n)

    cross.wait_recv()
    middle = (residual + (mine + head_in[...])).astype(BF).astype(F32)
    normed_two = rms_scaled(middle, gain_moe)
    outgoing = jnp.dot(pick_t, normed_two, preferred_element_type=F32)
    for c in range(cols):
        for k in range(2):
            wide_a[pl.ds(c * 2 + k, experts, stride=2 * cols), :] = outgoing[
                k * experts : (k + 1) * experts, c * hd : (c + 1) * hd
            ]
    disp_out[...] = wide_a[...].reshape(experts, 2 * cols, hd).astype(BF)
    to_all(lambda peer: disp_out.at[peer // 2], disp_in, 2)

    wait_bytes(q_in, recv_sems.at[0])
    served = owner_s[me]
    heads[last : last + 8, :] = q_in[served].astype(F32)
    attend(slots - 1, 1)
    late_terms = head_terms()[slots - 1 : slots, :]
    row_sum[...] = late_terms

    def row_copy():
        return pltpu.make_async_remote_copy(
            src_ref=row_sum,
            dst_ref=row_in,
            send_sem=r_send,
            recv_sem=r_recv,
            device_id=sibling,
        )

    @pl.when(first_core)
    def _():
        row_copy().start()

    l_wr.wait()

    def route_weights(normed_rows, chosen_by):
        logits = lax.dot_general(normed_rows, wr[...], LAST, preferred_element_type=F32)
        choice = lax.broadcasted_iota(jnp.int32, logits.shape, 1)
        chosen = [
            jnp.sum(jnp.where(choice == r[:, :experts], logits, 0.0), axis=-1, keepdims=True)
            for r in chosen_by
        ]
        best = functools.reduce(jnp.maximum, chosen)
        powers = [jnp.exp(c - best) for c in chosen]
        denom = functools.reduce(jnp.add, powers)
        blend = jnp.zeros((half, 128), F32)
        for r, power in zip(chosen_by, powers):
            blend = blend + jnp.where(r == peer_expert, power / denom, 0.0)
        return blend

    def in_parts(blend):
        part_a = blend.astype(BF).astype(F32)
        part_b = (blend - part_a).astype(BF).astype(F32)
        part_c = blend - part_a - part_b
        return jnp.concatenate([part_a, part_b, part_c], axis=0).astype(BF)

    def blended(parts, rows):
        mixed = jnp.dot(parts, rows, preferred_element_type=F32)
        return mixed[:half] + mixed[half : 2 * half] + mixed[2 * half :]

    blend_parts = in_parts(route_weights(normed_two, early) * peer_place)

    @pl.when(relocating)
    def _():
        wait_bytes(t_in, recv_sems.at[1])
        row_copy().wait_recv()
        total = row_sum[...] + row_in[...]
        for c in range(cols):
            m_wide[c : c + 1, :] = total[:, c * hd : (c + 1) * hd]
        m_out[...] = (t_in[served].astype(F32) + m_wide[...]).astype(BF)
        to_all(lambda peer: m_out, m_in, 3)

    def run_expert(rows):
        result = None
        for t in range(2):
            gate = lax.dot_general(rows, wg[t], LAST, preferred_element_type=F32)
            up = lax.dot_general(rows, wu[t], LAST, preferred_element_type=F32)
            hidden = (jnp.maximum(gate, 0.0) * up).astype(BF)
            part = jnp.dot(hidden, wd[t], preferred_element_type=F32)
            result = part if result is None else result + part
        return result

    def unpack(wide, first, stride):
        return jnp.concatenate(
            [wide[pl.ds(first(c), n, stride=stride), :] for c in range(cols)], axis=1
        )

    def unpack_pair():
        return jnp.concatenate(
            [unpack(wide_b, lambda c: c * 2 + k, 2 * cols).astype(BF) for k in range(2)], axis=0
        )

    l_wg.wait()
    l_wu.wait()
    l_wd.wait()
    for swap in swaps:
        swap.wait_recv()
    wait_bytes(disp_in, recv_sems.at[2])
    wide_b[...] = disp_in[...].astype(F32).reshape(n * 2 * cols, hd)
    result = run_expert(unpack_pair())
    for c in range(cols):
        for k in range(2):
            wide_b[pl.ds(c * 2 + k, n, stride=2 * cols), :] = result[
                k * n : (k + 1) * n, c * hd : (c + 1) * hd
            ]
    ret_out[...] = wide_b[...].reshape(n, 2 * cols, hd).astype(BF)
    to_all(lambda peer: ret_out.at[peer], ret_in, 4)

    @pl.when(relocating)
    def _():
        owners = jnp.zeros((8, 128), jnp.int32)
        owner_lane = lax.broadcasted_iota(jnp.int32, (8, 128), 1)
        for c in range(n):
            owners = jnp.where(owner_lane == c, owner_s[c], owners)
        slot_row = lax.broadcasted_iota(jnp.int32, (n, n), 0)
        moves = jnp.where(slot_row == owners[0:1, :n], 1.0, 0.0).astype(BF)
        wait_bytes(m_in, recv_sems.at[3])
        wide_m[...] = m_in[...].astype(F32).reshape(n * 16, hd)
        late_normed = rms_scaled(unpack(wide_m, lambda c: c, 16), gain_moe)
        ordered = jnp.dot(moves, late_normed, preferred_element_type=F32).astype(BF)
        late_result = run_expert(ordered)

        def find(c, found):
            return jnp.where(owner_s[c] == me, c, found)

        origin = lax.fori_loop(0, n, find, 0)
        late_middle = jnp.concatenate(
            [wide_m[pl.ds(origin * 16 + c, 1), :] for c in range(cols)], axis=1
        )
        late_middle = jnp.broadcast_to(late_middle, (half, width))
        late_blend = in_parts(
            jnp.where(
                lane < n,
                route_weights(rms_scaled(late_middle, gain_moe), route),
                0.0,
            )[:, :n]
        )
        for c in range(cols):
            wide_m[pl.ds(c, n, stride=16), :] = late_result[:, c * hd : (c + 1) * hd]
        late_out[...] = wide_m[...].reshape(n, 16, hd).astype(BF)
        to_all(lambda peer: late_out.at[peer], late_in, 5)
        wait_bytes(late_in, recv_sems.at[5])
        wide_m[...] = late_in[...].astype(F32).reshape(n * 16, hd)
        late = late_middle + blended(late_blend, unpack(wide_m, lambda c: c, 16).astype(BF))
        fin[half - 1 : half, :] = late[half - 1 : half, :]

    wait_bytes(ret_in, recv_sems.at[4])
    wide_b[...] = ret_in[...].astype(F32).reshape(n * 2 * cols, hd)
    done = middle + blended(blend_parts, unpack_pair())
    kept = (lax.broadcasted_iota(jnp.int32, (half, width), 0) == half - 1) & relocating
    out_ref[...] = jnp.where(kept, fin[...], done).astype(BF)

    cross.wait_send()
    for swap in swaps:
        swap.wait_send()
    for phase, ref in ((0, q_in), (2, disp_in), (4, ret_in)):
        wait_bytes(ref.at[pl.ds(0, n - 1)], send_sems.at[phase])

    @pl.when(first_core)
    def _():
        row_copy().wait_send()

    @pl.when(relocating)
    def _():
        for phase, ref in ((1, t_in), (3, m_in), (5, late_in)):
            wait_bytes(ref.at[pl.ds(0, n - 1)], send_sems.at[phase])


def solution(mesh):
    n = mesh.shape["req"]

    def shards(
        tokens,
        gain_attn,
        w_query,
        w_key,
        w_value,
        w_out,
        cache_k,
        cache_v,
        page_table,
        lengths,
        new_owner,
        gain_moe,
        w_router,
        routes,
        w_gate,
        w_up,
        w_down,
    ):
        slots, width = tokens.shape
        half = slots // 2
        hd = w_key.shape[1]
        cols = width // hd
        experts = n // 2
        span = page_table.shape[1] * cache_k.shape[1]
        hidden = w_gate.shape[2]
        hbm = pl.BlockSpec(memory_space=pl.ANY)
        dma = pltpu.SemaphoreType.DMA
        return pl.pallas_call(
            functools.partial(layer_kernel, n),
            out_shape=jax.ShapeDtypeStruct((half, width), BF),
            in_specs=[hbm] * 4 + [hbm] * 13,
            out_specs=pl.BlockSpec(memory_space=pltpu.VMEM),
            scratch_shapes=[
                pltpu.VMEM((slots, width), BF),
                pltpu.VMEM((width,), BF),
                pltpu.VMEM((width,), BF),
                pltpu.VMEM((width, w_query.shape[1] + 2 * hd), BF),
                pltpu.VMEM(w_out.shape, BF),
                pltpu.VMEM(cache_k.shape, BF),
                pltpu.VMEM(cache_v.shape, BF),
                pltpu.VMEM(w_router.shape[::-1], BF),
                pltpu.VMEM((2, hidden, width), BF),
                pltpu.VMEM((2, hidden, width), BF),
                pltpu.VMEM((2, hidden, width), BF),
                pltpu.VMEM((slots * 8, hd), F32),
                pltpu.VMEM((slots * 8, span), F32),
                pltpu.VMEM((slots * 8, hd), F32),
                pltpu.VMEM((8, hd), BF),
                pltpu.VMEM((n, 8, hd), BF),
                pltpu.VMEM((2, half, width), F32),
                pltpu.VMEM((half, width), F32),
                pltpu.VMEM((experts * 2 * cols, hd), F32),
                pltpu.VMEM((experts, 2 * cols, hd), BF),
                pltpu.VMEM((n, 2 * cols, hd), BF),
                pltpu.VMEM((n * 2 * cols, hd), F32),
                pltpu.VMEM((n, 2 * cols, hd), BF),
                pltpu.VMEM((n, 2 * cols, hd), BF),
                pltpu.SMEM(page_table.shape[::-1], jnp.int32),
                pltpu.SMEM(lengths.shape, jnp.int32),
                pltpu.SMEM(new_owner.shape, jnp.int32),
                pltpu.SMEM(routes.shape[::-1], jnp.int32),
                pltpu.VMEM((half, width), F32),
                pltpu.VMEM((1, width), F32),
                pltpu.VMEM((1, width), F32),
                pltpu.VMEM((16, hd), BF),
                pltpu.VMEM((n, 16, hd), BF),
                pltpu.VMEM((16, hd), F32),
                pltpu.VMEM((16, hd), BF),
                pltpu.VMEM((n, 16, hd), BF),
                pltpu.VMEM((n * 16, hd), F32),
                pltpu.VMEM((n, 16, hd), BF),
                pltpu.VMEM((n, 16, hd), BF),
                dma((17,)),
                dma((3,)),
                dma((3,)),
                dma,
                dma,
                dma,
                dma,
                dma((6,)),
                dma((6,)),
            ],
            compiler_params=pltpu.CompilerParams(
                collective_id=0, has_side_effects=True, vmem_limit_bytes=60 * 1024 * 1024
            ),
        )(
            page_table.T,
            lengths,
            new_owner,
            routes.T,
            tokens,
            gain_attn,
            gain_moe,
            w_query,
            w_key,
            w_value,
            w_out,
            cache_k,
            cache_v,
            w_router.T,
            jnp.swapaxes(w_gate, 1, 2),
            jnp.swapaxes(w_up, 1, 2),
            jnp.swapaxes(w_down, 1, 2),
        )

    return jax.shard_map(
        shards,
        mesh=mesh,
        in_specs=(
            P("req", None),
            P(),
            P(None, "kv"),
            P(None, "kv"),
            P(None, "kv"),
            P("kv", None),
            P("req", None, "kv"),
            P("req", None, "kv"),
            P("req", None),
            P(),
            P(),
            P(),
            P(),
            P(("req", "kv"), None),
            P("req", None, "kv"),
            P("req", None, "kv"),
            P("req", None, "kv"),
        ),
        out_specs=P(("req", "kv"), None),
        check_vma=False,
    )
```

```python
import functools
import itertools

import jax
import jax.numpy as jnp
from jax import lax
from jax.experimental import pallas as pl
from jax.experimental.pallas import tpu as pltpu
from jax.sharding import PartitionSpec as P

BF = jnp.bfloat16
F32 = jnp.float32
LAST = (((1,), (1,)), ((), ()))


def rms_scaled(wide, gain_row):
    squares = jnp.mean(wide * wide, axis=-1, keepdims=True)
    return (wide * lax.rsqrt(squares + 1e-06) * gain_row).astype(BF)


def wait_bytes(ref, sem):
    pltpu.make_async_copy(ref, ref, sem).wait()


def layer_kernel(
    n,
    pages_h,
    lengths_h,
    owner_h,
    routes_h,
    tokens_h,
    gain_a_h,
    gain_m_h,
    wq_h,
    wk_h,
    wv_h,
    wo_h,
    ck_h,
    cv_h,
    wr_h,
    wg_h,
    wu_h,
    wd_h,
    out_ref,
    tok,
    gain_a,
    gain_m,
    wqkv,
    wo,
    ck,
    cv,
    wr,
    wg,
    wu,
    wd,
    heads,
    scores,
    att,
    q_out,
    q_in,
    head_sum,
    head_in,
    wide_a,
    disp_out,
    disp_in,
    wide_b,
    ret_out,
    ret_in,
    pages_s,
    lengths_s,
    owner_s,
    routes_s,
    fin,
    row_sum,
    row_in,
    t_out,
    t_in,
    m_wide,
    m_out,
    m_in,
    wide_m,
    late_out,
    late_in,
    load_sems,
    w_send,
    w_recv,
    h_send,
    h_recv,
    r_send,
    r_recv,
    send_sems,
    recv_sems,
):
    me = lax.axis_index("req")
    kv = lax.axis_index("kv")
    slots, width = tok.shape
    half = slots // 2
    hd = ck.shape[2]
    page = ck.shape[1]
    per_slot = pages_s.shape[0]
    groups = wo.shape[0] // hd
    experts = n // 2
    cols = width // hd
    inv_root = hd ** (-0.5)

    def load(src, dst, i):
        copy = pltpu.make_async_copy(src, dst, load_sems.at[i])
        copy.start()
        return copy

    qcols = wq_h.shape[1]
    l_tok = load(tokens_h, tok, 0)
    l_gain = load(gain_a_h, gain_a, 1)
    l_gain_m = load(gain_m_h, gain_m, 12)
    l_wq = load(wq_h, wqkv.at[:, pl.ds(0, qcols)], 2)
    l_wk = load(wk_h, wqkv.at[:, pl.ds(qcols, hd)], 3)
    l_wv = load(wv_h, wqkv.at[:, pl.ds(qcols + hd, hd)], 4)

    sibling = {"kv": 1 - kv}
    relocating = kv == 1
    barrier = pltpu.get_barrier_semaphore()

    def greet(i, carry):
        pl.semaphore_signal(barrier, 1, device_id={"req": lax.rem(me + i, n)})
        return carry

    pl.semaphore_signal(barrier, 1, device_id=sibling)
    lax.fori_loop(1, n, greet, 0)
    l_ints = [
        load(src, dst, 13 + i)
        for i, (src, dst) in enumerate(
            (
                (pages_h, pages_s),
                (lengths_h, lengths_s),
                (owner_h, owner_s),
                (routes_h, routes_s),
            )
        )
    ]
    l_ck = load(ck_h, ck, 5)
    l_cv = load(cv_h, cv, 6)
    l_wo = load(wo_h, wo, 7)
    l_wr = load(wr_h, wr, 8)
    l_wg = load(wg_h.at[0], wg.at[0], 9)
    l_wu = load(wu_h.at[0], wu.at[0], 10)
    l_wd = load(wd_h.at[0], wd.at[0], 11)

    side = round(n ** (1 / 3))
    me_z, me_x, me_y = me // (side * side), lax.rem(me // side, side), lax.rem(me, side)
    at_z = [lax.rem(me_z + d, side) * (side * side) for d in range(side)]
    at_x = [lax.rem(me_x + d, side) * side for d in range(side)]
    at_y = [lax.rem(me_y + d, side) for d in range(side)]

    def hops(offset):
        return sum(min(d, side - d) for d in offset)

    offsets = sorted(
        (o for o in itertools.product(range(side), repeat=3) if any(o)), key=lambda o: -hops(o)
    )

    def to_all(src_of, dst, phase):
        for dz, dx, dy in offsets:
            peer = at_z[dz] + at_x[dx] + at_y[dy]
            pltpu.make_async_remote_copy(
                src_ref=src_of(peer),
                dst_ref=dst.at[me],
                send_sem=send_sems.at[phase],
                recv_sem=recv_sems.at[phase],
                device_id={"req": peer},
            ).start()
        pltpu.make_async_copy(src_of(me), dst.at[me], recv_sems.at[phase]).start()

    l_tok.wait()
    l_gain.wait()
    l_gain_m.wait()
    gain_attn = gain_a[...].astype(F32).reshape(1, width)
    gain_moe = gain_m[...].astype(F32).reshape(1, width)
    tokf = tok[...].astype(F32)
    normed = rms_scaled(tokf, gain_attn)
    last = (slots - 1) * 8
    m_wide[...] = jnp.zeros((16, hd), F32)
    for c in range(cols):
        m_wide[c : c + 1, :] = tokf[slots - 1 : slots, c * hd : (c + 1) * hd]
    t_out[...] = m_wide[...].astype(BF)
    l_wq.wait()
    l_wk.wait()
    l_wv.wait()
    qkv = jnp.dot(normed, wqkv[...], preferred_element_type=F32).astype(BF).astype(F32)
    for h in range(groups + 2):
        heads[pl.ds(h, slots, stride=8), :] = qkv[:, h * hd : (h + 1) * hd]
    q_out[...] = heads[last : last + 8, :].astype(BF)
    pl.semaphore_wait(barrier, n)
    to_all(lambda peer: q_out, q_in, 0)

    @pl.when(relocating)
    def _():
        to_all(lambda peer: t_out, t_in, 1)

    swaps = []
    for i, (src, dst) in enumerate(((wg_h, wg), (wu_h, wu), (wd_h, wd))):
        swap = pltpu.make_async_remote_copy(
            src_ref=src.at[0],
            dst_ref=dst.at[1],
            send_sem=w_send.at[i],
            recv_sem=w_recv.at[i],
            device_id=sibling,
        )
        swap.start()
        swaps.append(swap)

    def attend(first, count):
        rows = slice(first * 8, (first + count) * 8)
        place = lax.broadcasted_iota(jnp.int32, (8, page), 1)
        for s in range(first, first + count):
            block = heads[s * 8 : s * 8 + 8, :].astype(BF)
            live = lengths_s[me * slots + s]
            for j in range(per_slot):
                dots = lax.dot_general(
                    block, ck[pages_s[j, s]], LAST, preferred_element_type=F32
                )
                scores[s * 8 : s * 8 + 8, j * page : (j + 1) * page] = jnp.where(
                    place + j * page < live, dots * inv_root, -1e30
                )
        all_scores = scores[rows, :]
        top = jnp.max(all_scores, axis=-1, keepdims=True)
        weights = jnp.exp(all_scores - top)
        total = jnp.sum(weights, axis=-1, keepdims=True)
        scores[rows, :] = weights
        for s in range(first, first + count):
            acc = jnp.zeros((8, hd), F32)
            for j in range(per_slot):
                acc = acc + jnp.dot(
                    scores[s * 8 : s * 8 + 8, j * page : (j + 1) * page].astype(BF),
                    cv[pages_s[j, s]],
                    preferred_element_type=F32,
                )
            att[s * 8 : s * 8 + 8, :] = acc
        block = heads[rows, :].reshape(count, 8, hd)
        own = jnp.sum(block * block[:, groups : groups + 1, :], axis=-1, keepdims=True) * inv_root
        top = top.reshape(count, 8, 1)
        total = total.reshape(count, 8, 1)
        joint = jnp.maximum(top, own)
        old_part = jnp.exp(top - joint)
        new_part = jnp.exp(own - joint)
        merged = (
            att[rows, :].reshape(count, 8, hd) * old_part
            + new_part * block[:, groups + 1 : groups + 2, :]
        )
        result = merged / (total * old_part + new_part)
        att[rows, :] = result.astype(BF).astype(F32).reshape(count * 8, hd)

    for l_int in l_ints:
        l_int.wait()
    l_ck.wait()
    l_cv.wait()
    attend(0, slots - 1)
    att[last : last + 8, :] = jnp.zeros((8, hd), F32)
    l_wo.wait()

    def head_terms():
        attended = jnp.concatenate(
            [att[pl.ds(h, slots, stride=8), :].astype(BF) for h in range(groups)], axis=1
        )
        return jnp.dot(attended, wo[...], preferred_element_type=F32)

    terms = head_terms()
    head_sum[0] = terms[:half]
    head_sum[1] = terms[half:]
    cross = pltpu.make_async_remote_copy(
        src_ref=head_sum.at[1 - kv],
        dst_ref=head_in,
        send_sem=h_send,
        recv_sem=h_recv,
        device_id=sibling,
    )
    cross.start()
    first_core = kv == 0
    mine = jnp.where(first_core, terms[:half], terms[half:])
    residual = jnp.where(first_core, tokf[:half], tokf[half:])

    topk = routes_s.shape[0]
    lane = lax.broadcasted_iota(jnp.int32, (half, 128), 1)
    row = lax.broadcasted_iota(jnp.int32, (half, 128), 0)
    late_row = (row == half - 1) & relocating
    route = []
    for j in range(topk):
        named_by = jnp.zeros((half, 128), jnp.int32)
        for i in range(half):
            named_by = jnp.where(row == i, routes_s[j, i], named_by)
        route.append(named_by)
    early = [jnp.where(late_row, -1, r) for r in route]

    def places(expert, slot):
        named = jnp.zeros((half, 128), F32)
        for j in range(topk):
            named = named + jnp.where(early[j] == expert, 1.0, 0.0)
        rank = jnp.zeros((half, 128), F32)
        for i in range(half - 1):
            rank = rank + jnp.where(row > i, named[i : i + 1, :], 0.0)
        return jnp.where(rank == slot.astype(F32), named, 0.0)

    pick = places(lane % experts, lane // experts)
    pick_t = jnp.transpose(pick)[: 2 * experts, :].astype(BF)
    peer_expert = (lane % n) // 2
    peer_place = places(peer_expert, lane // n)

    cross.wait_recv()
    middle = (residual + (mine + head_in[...])).astype(BF).astype(F32)
    normed_two = rms_scaled(middle, gain_moe)
    outgoing = jnp.dot(pick_t, normed_two, preferred_element_type=F32)
    for c in range(cols):
        for k in range(2):
            wide_a[pl.ds(c * 2 + k, experts, stride=2 * cols), :] = outgoing[
                k * experts : (k + 1) * experts, c * hd : (c + 1) * hd
            ]
    disp_out[...] = wide_a[...].reshape(experts, 2 * cols, hd).astype(BF)
    to_all(lambda peer: disp_out.at[peer // 2], disp_in, 2)

    wait_bytes(q_in, recv_sems.at[0])
    served = owner_s[me]
    heads[last : last + 8, :] = q_in[served].astype(F32)
    attend(slots - 1, 1)
    late_terms = head_terms()[slots - 1 : slots, :]
    row_sum[...] = late_terms

    def row_copy():
        return pltpu.make_async_remote_copy(
            src_ref=row_sum,
            dst_ref=row_in,
            send_sem=r_send,
            recv_sem=r_recv,
            device_id=sibling,
        )

    @pl.when(first_core)
    def _():
        row_copy().start()

    l_wr.wait()

    def route_weights(normed_rows, chosen_by):
        logits = lax.dot_general(normed_rows, wr[...], LAST, preferred_element_type=F32)
        choice = lax.broadcasted_iota(jnp.int32, logits.shape, 1)
        chosen = [
            jnp.sum(jnp.where(choice == r[:, :experts], logits, 0.0), axis=-1, keepdims=True)
            for r in chosen_by
        ]
        best = functools.reduce(jnp.maximum, chosen)
        powers = [jnp.exp(c - best) for c in chosen]
        denom = functools.reduce(jnp.add, powers)
        blend = jnp.zeros((half, 128), F32)
        for r, power in zip(chosen_by, powers):
            blend = blend + jnp.where(r == peer_expert, power / denom, 0.0)
        return blend

    def in_parts(blend):
        part_a = blend.astype(BF).astype(F32)
        part_b = (blend - part_a).astype(BF).astype(F32)
        part_c = blend - part_a - part_b
        return jnp.concatenate([part_a, part_b, part_c], axis=0).astype(BF)

    def blended(parts, rows):
        mixed = jnp.dot(parts, rows, preferred_element_type=F32)
        return mixed[:half] + mixed[half : 2 * half] + mixed[2 * half :]

    blend_parts = in_parts(route_weights(normed_two, early) * peer_place)

    @pl.when(relocating)
    def _():
        wait_bytes(t_in, recv_sems.at[1])
        row_copy().wait_recv()
        total = row_sum[...] + row_in[...]
        for c in range(cols):
            m_wide[c : c + 1, :] = total[:, c * hd : (c + 1) * hd]
        m_out[...] = (t_in[served].astype(F32) + m_wide[...]).astype(BF)
        to_all(lambda peer: m_out, m_in, 3)

    def run_expert(rows):
        result = None
        for t in range(2):
            gate = lax.dot_general(rows, wg[t], LAST, preferred_element_type=F32)
            up = lax.dot_general(rows, wu[t], LAST, preferred_element_type=F32)
            hidden = (jnp.maximum(gate, 0.0) * up).astype(BF)
            part = jnp.dot(hidden, wd[t], preferred_element_type=F32)
            result = part if result is None else result + part
        return result

    def unpack(wide, first, stride):
        return jnp.concatenate(
            [wide[pl.ds(first(c), n, stride=stride), :] for c in range(cols)], axis=1
        )

    def unpack_pair():
        return jnp.concatenate(
            [unpack(wide_b, lambda c: c * 2 + k, 2 * cols).astype(BF) for k in range(2)], axis=0
        )

    l_wg.wait()
    l_wu.wait()
    l_wd.wait()
    for swap in swaps:
        swap.wait_recv()
    wait_bytes(disp_in, recv_sems.at[2])
    wide_b[...] = disp_in[...].astype(F32).reshape(n * 2 * cols, hd)
    result = run_expert(unpack_pair())
    for c in range(cols):
        for k in range(2):
            wide_b[pl.ds(c * 2 + k, n, stride=2 * cols), :] = result[
                k * n : (k + 1) * n, c * hd : (c + 1) * hd
            ]
    ret_out[...] = wide_b[...].reshape(n, 2 * cols, hd).astype(BF)
    to_all(lambda peer: ret_out.at[peer], ret_in, 4)

    @pl.when(relocating)
    def _():
        owners = jnp.zeros((8, 128), jnp.int32)
        owner_lane = lax.broadcasted_iota(jnp.int32, (8, 128), 1)
        for c in range(n):
            owners = jnp.where(owner_lane == c, owner_s[c], owners)
        slot_row = lax.broadcasted_iota(jnp.int32, (n, n), 0)
        moves = jnp.where(slot_row == owners[0:1, :n], 1.0, 0.0).astype(BF)
        wait_bytes(m_in, recv_sems.at[3])
        wide_m[...] = m_in[...].astype(F32).reshape(n * 16, hd)
        late_normed = rms_scaled(unpack(wide_m, lambda c: c, 16), gain_moe)
        ordered = jnp.dot(moves, late_normed, preferred_element_type=F32).astype(BF)
        late_result = run_expert(ordered)

        def find(c, found):
            return jnp.where(owner_s[c] == me, c, found)

        origin = lax.fori_loop(0, n, find, 0)
        late_middle = jnp.concatenate(
            [wide_m[pl.ds(origin * 16 + c, 1), :] for c in range(cols)], axis=1
        )
        late_middle = jnp.broadcast_to(late_middle, (half, width))
        late_blend = in_parts(
            jnp.where(
                lane < n,
                route_weights(rms_scaled(late_middle, gain_moe), route),
                0.0,
            )[:, :n]
        )
        for c in range(cols):
            wide_m[pl.ds(c, n, stride=16), :] = late_result[:, c * hd : (c + 1) * hd]
        late_out[...] = wide_m[...].reshape(n, 16, hd).astype(BF)
        to_all(lambda peer: late_out.at[peer], late_in, 5)
        wait_bytes(late_in, recv_sems.at[5])
        wide_m[...] = late_in[...].astype(F32).reshape(n * 16, hd)
        late = late_middle + blended(late_blend, unpack(wide_m, lambda c: c, 16).astype(BF))
        fin[half - 1 : half, :] = late[half - 1 : half, :]

    wait_bytes(ret_in, recv_sems.at[4])
    wide_b[...] = ret_in[...].astype(F32).reshape(n * 2 * cols, hd)
    done = middle + blended(blend_parts, unpack_pair())
    kept = (lax.broadcasted_iota(jnp.int32, (half, width), 0) == half - 1) & relocating
    out_ref[...] = jnp.where(kept, fin[...], done).astype(BF)

    cross.wait_send()
    for swap in swaps:
        swap.wait_send()
    for phase, ref in ((0, q_in), (2, disp_in), (4, ret_in)):
        wait_bytes(ref.at[pl.ds(0, n - 1)], send_sems.at[phase])

    @pl.when(first_core)
    def _():
        row_copy().wait_send()

    @pl.when(relocating)
    def _():
        for phase, ref in ((1, t_in), (3, m_in), (5, late_in)):
            wait_bytes(ref.at[pl.ds(0, n - 1)], send_sems.at[phase])


def solution(mesh):
    n = mesh.shape["req"]

    def shards(
        tokens,
        gain_attn,
        w_query,
        w_key,
        w_value,
        w_out,
        cache_k,
        cache_v,
        page_table,
        lengths,
        new_owner,
        gain_moe,
        w_router,
        routes,
        w_gate,
        w_up,
        w_down,
    ):
        slots, width = tokens.shape
        half = slots // 2
        hd = w_key.shape[1]
        cols = width // hd
        experts = n // 2
        span = page_table.shape[1] * cache_k.shape[1]
        hidden = w_gate.shape[2]
        hbm = pl.BlockSpec(memory_space=pl.ANY)
        dma = pltpu.SemaphoreType.DMA
        return pl.pallas_call(
            functools.partial(layer_kernel, n),
            out_shape=pltpu.VMEM((half, width), BF),
            in_specs=[hbm] * 4 + [hbm] * 13,
            out_specs=pl.BlockSpec(memory_space=pltpu.VMEM),
            scratch_shapes=[
                pltpu.VMEM((slots, width), BF),
                pltpu.VMEM((width,), BF),
                pltpu.VMEM((width,), BF),
                pltpu.VMEM((width, w_query.shape[1] + 2 * hd), BF),
                pltpu.VMEM(w_out.shape, BF),
                pltpu.VMEM(cache_k.shape, BF),
                pltpu.VMEM(cache_v.shape, BF),
                pltpu.VMEM(w_router.shape[::-1], BF),
                pltpu.VMEM((2, hidden, width), BF),
                pltpu.VMEM((2, hidden, width), BF),
                pltpu.VMEM((2, hidden, width), BF),
                pltpu.VMEM((slots * 8, hd), F32),
                pltpu.VMEM((slots * 8, span), F32),
                pltpu.VMEM((slots * 8, hd), F32),
                pltpu.VMEM((8, hd), BF),
                pltpu.VMEM((n, 8, hd), BF),
                pltpu.VMEM((2, half, width), F32),
                pltpu.VMEM((half, width), F32),
                pltpu.VMEM((experts * 2 * cols, hd), F32),
                pltpu.VMEM((experts, 2 * cols, hd), BF),
                pltpu.VMEM((n, 2 * cols, hd), BF),
                pltpu.VMEM((n * 2 * cols, hd), F32),
                pltpu.VMEM((n, 2 * cols, hd), BF),
                pltpu.VMEM((n, 2 * cols, hd), BF),
                pltpu.SMEM(page_table.shape[::-1], jnp.int32),
                pltpu.SMEM(lengths.shape, jnp.int32),
                pltpu.SMEM(new_owner.shape, jnp.int32),
                pltpu.SMEM(routes.shape[::-1], jnp.int32),
                pltpu.VMEM((half, width), F32),
                pltpu.VMEM((1, width), F32),
                pltpu.VMEM((1, width), F32),
                pltpu.VMEM((16, hd), BF),
                pltpu.VMEM((n, 16, hd), BF),
                pltpu.VMEM((16, hd), F32),
                pltpu.VMEM((16, hd), BF),
                pltpu.VMEM((n, 16, hd), BF),
                pltpu.VMEM((n * 16, hd), F32),
                pltpu.VMEM((n, 16, hd), BF),
                pltpu.VMEM((n, 16, hd), BF),
                dma((17,)),
                dma((3,)),
                dma((3,)),
                dma,
                dma,
                dma,
                dma,
                dma((6,)),
                dma((6,)),
            ],
            compiler_params=pltpu.CompilerParams(
                collective_id=0, has_side_effects=True, vmem_limit_bytes=60 * 1024 * 1024
            ),
        )(
            page_table.T,
            lengths,
            new_owner,
            routes.T,
            tokens,
            gain_attn,
            gain_moe,
            w_query,
            w_key,
            w_value,
            w_out,
            cache_k,
            cache_v,
            w_router.T,
            jnp.swapaxes(w_gate, 1, 2),
            jnp.swapaxes(w_up, 1, 2),
            jnp.swapaxes(w_down, 1, 2),
        )

    return jax.shard_map(
        shards,
        mesh=mesh,
        in_specs=(
            P("req", None),
            P(),
            P(None, "kv"),
            P(None, "kv"),
            P(None, "kv"),
            P("kv", None),
            P("req", None, "kv"),
            P("req", None, "kv"),
            P("req", None),
            P(),
            P(),
            P(),
            P(),
            P(("req", "kv"), None),
            P("req", None, "kv"),
            P("req", None, "kv"),
            P("req", None, "kv"),
        ),
        out_specs=P(("req", "kv"), None),
        check_vma=False,
    )
```

```python
import functools
import itertools

import jax
import jax.numpy as jnp
from jax import lax
from jax.experimental import pallas as pl
from jax.experimental.pallas import tpu as pltpu
from jax.sharding import PartitionSpec as P

BF = jnp.bfloat16
F32 = jnp.float32
LAST = (((1,), (1,)), ((), ()))


def rms_scaled(wide, gain_row):
    squares = jnp.mean(wide * wide, axis=-1, keepdims=True)
    return (wide * lax.rsqrt(squares + 1e-06) * gain_row).astype(BF)


def wait_bytes(ref, sem):
    pltpu.make_async_copy(ref, ref, sem).wait()


def layer_kernel(
    n,
    pages_h,
    lengths_h,
    owner_h,
    routes_h,
    tokens_h,
    gain_a_h,
    gain_m_h,
    wq_h,
    wk_h,
    wv_h,
    wo_h,
    ck_h,
    cv_h,
    wr_h,
    wg_h,
    wu_h,
    wd_h,
    out_ref,
    tok,
    gain_a,
    gain_m,
    wqkv,
    wo,
    ck,
    cv,
    wr,
    wg,
    wu,
    wd,
    heads,
    scores,
    att,
    q_out,
    q_in,
    head_sum,
    head_in,
    wide_a,
    disp_out,
    disp_in,
    wide_b,
    ret_out,
    ret_in,
    pages_s,
    lengths_s,
    owner_s,
    routes_s,
    fin,
    row_sum,
    row_in,
    t_out,
    t_in,
    m_wide,
    m_out,
    m_in,
    wide_m,
    late_out,
    late_in,
    load_sems,
    w_send,
    w_recv,
    h_send,
    h_recv,
    r_send,
    r_recv,
    send_sems,
    recv_sems,
):
    me = lax.axis_index("req")
    kv = lax.axis_index("kv")
    slots, width = tok.shape
    half = slots // 2
    hd = ck.shape[2]
    page = ck.shape[1]
    per_slot = pages_s.shape[0]
    groups = wo.shape[0] // hd
    experts = n // 2
    cols = width // hd
    inv_root = hd ** (-0.5)

    side = round(n ** (1 / 3))
    me_z, me_x, me_y = me // (side * side), lax.rem(me // side, side), lax.rem(me, side)
    at_z = [lax.rem(me_z + d, side) * (side * side) for d in range(side)]
    at_x = [lax.rem(me_x + d, side) * side for d in range(side)]
    at_y = [lax.rem(me_y + d, side) for d in range(side)]

    def hops(offset):
        return sum(min(d, side - d) for d in offset)

    offsets = sorted(
        (o for o in itertools.product(range(side), repeat=3) if any(o)), key=lambda o: -hops(o)
    )

    def shifted(offset):
        dz, dx, dy = offset
        return at_z[dz] + at_x[dx] + at_y[dy]

    sibling = {"kv": 1 - kv}
    relocating = kv == 1
    barrier = pltpu.get_barrier_semaphore()
    for offset in offsets:
        pl.semaphore_signal(barrier, 1, device_id={"req": shifted(offset)})
    pl.semaphore_signal(barrier, 1, device_id=sibling)

    def load(src, dst, i):
        copy = pltpu.make_async_copy(src, dst, load_sems.at[i])
        copy.start()
        return copy

    qcols = wq_h.shape[1]
    l_tok = load(tokens_h, tok, 0)
    l_gain = load(gain_a_h, gain_a, 1)
    l_gain_m = load(gain_m_h, gain_m, 12)
    l_wq = load(wq_h, wqkv.at[:, pl.ds(0, qcols)], 2)
    l_wk = load(wk_h, wqkv.at[:, pl.ds(qcols, hd)], 3)
    l_wv = load(wv_h, wqkv.at[:, pl.ds(qcols + hd, hd)], 4)

    l_ints = [
        load(src, dst, 13 + i)
        for i, (src, dst) in enumerate(
            (
                (pages_h, pages_s),
                (lengths_h, lengths_s),
                (owner_h, owner_s),
                (routes_h, routes_s),
            )
        )
    ]
    l_ck = load(ck_h, ck, 5)
    l_cv = load(cv_h, cv, 6)
    l_wo = load(wo_h, wo, 7)
    l_wr = load(wr_h, wr, 8)
    l_wg = load(wg_h.at[0], wg.at[0], 9)
    l_wu = load(wu_h.at[0], wu.at[0], 10)
    l_wd = load(wd_h.at[0], wd.at[0], 11)

    def to_all(src_of, dst, phase):
        for offset in offsets:
            peer = shifted(offset)
            pltpu.make_async_remote_copy(
                src_ref=src_of(peer),
                dst_ref=dst.at[me],
                send_sem=send_sems.at[phase],
                recv_sem=recv_sems.at[phase],
                device_id={"req": peer},
            ).start()
        pltpu.make_async_copy(src_of(me), dst.at[me], recv_sems.at[phase]).start()

    l_tok.wait()
    l_gain.wait()
    l_gain_m.wait()
    gain_attn = gain_a[...].astype(F32).reshape(1, width)
    gain_moe = gain_m[...].astype(F32).reshape(1, width)
    tokf = tok[...].astype(F32)
    normed = rms_scaled(tokf, gain_attn)
    last = (slots - 1) * 8
    m_wide[...] = jnp.zeros((16, hd), F32)
    for c in range(cols):
        m_wide[c : c + 1, :] = tokf[slots - 1 : slots, c * hd : (c + 1) * hd]
    t_out[...] = m_wide[...].astype(BF)
    l_wq.wait()
    l_wk.wait()
    l_wv.wait()
    qkv = jnp.dot(normed, wqkv[...], preferred_element_type=F32).astype(BF).astype(F32)
    for h in range(groups + 2):
        heads[pl.ds(h, slots, stride=8), :] = qkv[:, h * hd : (h + 1) * hd]
    q_out[...] = heads[last : last + 8, :].astype(BF)
    pl.semaphore_wait(barrier, n)
    to_all(lambda peer: q_out, q_in, 0)

    @pl.when(relocating)
    def _():
        to_all(lambda peer: t_out, t_in, 1)

    def attend(first, count):
        rows = slice(first * 8, (first + count) * 8)
        place = lax.broadcasted_iota(jnp.int32, (8, page), 1)
        for s in range(first, first + count):
            block = heads[s * 8 : s * 8 + 8, :].astype(BF)
            live = lengths_s[me * slots + s]
            for j in range(per_slot):
                dots = lax.dot_general(
                    block, ck[pages_s[j, s]], LAST, preferred_element_type=F32
                )
                scores[s * 8 : s * 8 + 8, j * page : (j + 1) * page] = jnp.where(
                    place + j * page < live, dots * inv_root, -1e30
                )
        all_scores = scores[rows, :]
        top = jnp.max(all_scores, axis=-1, keepdims=True)
        weights = jnp.exp(all_scores - top)
        total = jnp.sum(weights, axis=-1, keepdims=True)
        scores[rows, :] = weights
        for s in range(first, first + count):
            acc = jnp.zeros((8, hd), F32)
            for j in range(per_slot):
                acc = acc + jnp.dot(
                    scores[s * 8 : s * 8 + 8, j * page : (j + 1) * page].astype(BF),
                    cv[pages_s[j, s]],
                    preferred_element_type=F32,
                )
            att[s * 8 : s * 8 + 8, :] = acc
        block = heads[rows, :].reshape(count, 8, hd)
        own = jnp.sum(block * block[:, groups : groups + 1, :], axis=-1, keepdims=True) * inv_root
        top = top.reshape(count, 8, 1)
        total = total.reshape(count, 8, 1)
        joint = jnp.maximum(top, own)
        old_part = jnp.exp(top - joint)
        new_part = jnp.exp(own - joint)
        merged = (
            att[rows, :].reshape(count, 8, hd) * old_part
            + new_part * block[:, groups + 1 : groups + 2, :]
        )
        result = merged / (total * old_part + new_part)
        att[rows, :] = result.astype(BF).astype(F32).reshape(count * 8, hd)

    for l_int in l_ints:
        l_int.wait()
    l_ck.wait()
    l_cv.wait()
    attend(0, slots - 1)
    att[last : last + 8, :] = jnp.zeros((8, hd), F32)
    l_wo.wait()

    def head_terms():
        attended = jnp.concatenate(
            [att[pl.ds(h, slots, stride=8), :].astype(BF) for h in range(groups)], axis=1
        )
        return jnp.dot(attended, wo[...], preferred_element_type=F32)

    terms = head_terms()
    head_sum[0] = terms[:half]
    head_sum[1] = terms[half:]
    cross = pltpu.make_async_remote_copy(
        src_ref=head_sum.at[1 - kv],
        dst_ref=head_in,
        send_sem=h_send,
        recv_sem=h_recv,
        device_id=sibling,
    )
    cross.start()
    first_core = kv == 0
    mine = jnp.where(first_core, terms[:half], terms[half:])
    residual = jnp.where(first_core, tokf[:half], tokf[half:])

    topk = routes_s.shape[0]
    lane = lax.broadcasted_iota(jnp.int32, (half, 128), 1)
    row = lax.broadcasted_iota(jnp.int32, (half, 128), 0)
    late_row = (row == half - 1) & relocating
    route = []
    for j in range(topk):
        named_by = jnp.zeros((half, 128), jnp.int32)
        for i in range(half):
            named_by = jnp.where(row == i, routes_s[j, i], named_by)
        route.append(named_by)
    early = [jnp.where(late_row, -1, r) for r in route]

    def places(expert, slot):
        named = jnp.zeros((half, 128), F32)
        for j in range(topk):
            named = named + jnp.where(early[j] == expert, 1.0, 0.0)
        rank = jnp.zeros((half, 128), F32)
        for i in range(half - 1):
            rank = rank + jnp.where(row > i, named[i : i + 1, :], 0.0)
        return jnp.where(rank == slot.astype(F32), named, 0.0)

    pick = places(lane % experts, lane // experts)
    pick_t = jnp.transpose(pick)[: 2 * experts, :].astype(BF)
    peer_expert = (lane % n) // 2
    peer_place = places(peer_expert, lane // n)

    cross.wait_recv()
    middle = (residual + (mine + head_in[...])).astype(BF).astype(F32)
    normed_two = rms_scaled(middle, gain_moe)
    outgoing = jnp.dot(pick_t, normed_two, preferred_element_type=F32)
    for c in range(cols):
        for k in range(2):
            wide_a[pl.ds(c * 2 + k, experts, stride=2 * cols), :] = outgoing[
                k * experts : (k + 1) * experts, c * hd : (c + 1) * hd
            ]
    disp_out[...] = wide_a[...].reshape(experts, 2 * cols, hd).astype(BF)
    to_all(lambda peer: disp_out.at[peer // 2], disp_in, 2)
    swaps = []
    for i, (src, dst) in enumerate(((wg_h, wg), (wu_h, wu), (wd_h, wd))):
        swap = pltpu.make_async_remote_copy(
            src_ref=src.at[0],
            dst_ref=dst.at[1],
            send_sem=w_send.at[i],
            recv_sem=w_recv.at[i],
            device_id=sibling,
        )
        swap.start()
        swaps.append(swap)

    wait_bytes(q_in, recv_sems.at[0])
    served = owner_s[me]
    heads[last : last + 8, :] = q_in[served].astype(F32)
    attend(slots - 1, 1)
    late_terms = head_terms()[slots - 1 : slots, :]
    row_sum[...] = late_terms

    def row_copy():
        return pltpu.make_async_remote_copy(
            src_ref=row_sum,
            dst_ref=row_in,
            send_sem=r_send,
            recv_sem=r_recv,
            device_id=sibling,
        )

    @pl.when(first_core)
    def _():
        row_copy().start()

    l_wr.wait()

    def route_weights(normed_rows, chosen_by):
        logits = lax.dot_general(normed_rows, wr[...], LAST, preferred_element_type=F32)
        choice = lax.broadcasted_iota(jnp.int32, logits.shape, 1)
        chosen = [
            jnp.sum(jnp.where(choice == r[:, :experts], logits, 0.0), axis=-1, keepdims=True)
            for r in chosen_by
        ]
        best = functools.reduce(jnp.maximum, chosen)
        powers = [jnp.exp(c - best) for c in chosen]
        denom = functools.reduce(jnp.add, powers)
        blend = jnp.zeros((half, 128), F32)
        for r, power in zip(chosen_by, powers):
            blend = blend + jnp.where(r == peer_expert, power / denom, 0.0)
        return blend

    def in_parts(blend):
        part_a = blend.astype(BF).astype(F32)
        part_b = (blend - part_a).astype(BF).astype(F32)
        part_c = blend - part_a - part_b
        return jnp.concatenate([part_a, part_b, part_c], axis=0).astype(BF)

    def blended(parts, rows):
        mixed = jnp.dot(parts, rows, preferred_element_type=F32)
        return mixed[:half] + mixed[half : 2 * half] + mixed[2 * half :]

    blend_parts = in_parts(route_weights(normed_two, early) * peer_place)

    @pl.when(relocating)
    def _():
        wait_bytes(t_in, recv_sems.at[1])
        row_copy().wait_recv()
        total = row_sum[...] + row_in[...]
        for c in range(cols):
            m_wide[c : c + 1, :] = total[:, c * hd : (c + 1) * hd]
        m_out[...] = (t_in[served].astype(F32) + m_wide[...]).astype(BF)
        to_all(lambda peer: m_out, m_in, 3)

    def run_expert(rows):
        result = None
        for t in range(2):
            gate = lax.dot_general(rows, wg[t], LAST, preferred_element_type=F32)
            up = lax.dot_general(rows, wu[t], LAST, preferred_element_type=F32)
            hidden = (jnp.maximum(gate, 0.0) * up).astype(BF)
            part = jnp.dot(hidden, wd[t], preferred_element_type=F32)
            result = part if result is None else result + part
        return result

    def unpack(wide, first, stride):
        return jnp.concatenate(
            [wide[pl.ds(first(c), n, stride=stride), :] for c in range(cols)], axis=1
        )

    def unpack_pair():
        return jnp.concatenate(
            [unpack(wide_b, lambda c: c * 2 + k, 2 * cols).astype(BF) for k in range(2)], axis=0
        )

    owners = jnp.zeros((8, 128), jnp.int32)
    owner_lane = lax.broadcasted_iota(jnp.int32, (8, 128), 1)
    for c in range(n):
        owners = jnp.where(owner_lane == c, owner_s[c], owners)
    slot_row = lax.broadcasted_iota(jnp.int32, (n, n), 0)
    moves = jnp.where(slot_row == owners[0:1, :n], 1.0, 0.0).astype(BF)

    def find(c, found):
        return jnp.where(owner_s[c] == me, c, found)

    origin = lax.fori_loop(0, n, find, 0)
    l_wg.wait()
    l_wu.wait()
    l_wd.wait()
    for swap in swaps:
        swap.wait_recv()
    wait_bytes(disp_in, recv_sems.at[2])
    wide_b[...] = disp_in[...].astype(F32).reshape(n * 2 * cols, hd)
    result = run_expert(unpack_pair())
    for c in range(cols):
        for k in range(2):
            wide_b[pl.ds(c * 2 + k, n, stride=2 * cols), :] = result[
                k * n : (k + 1) * n, c * hd : (c + 1) * hd
            ]
    ret_out[...] = wide_b[...].reshape(n, 2 * cols, hd).astype(BF)
    to_all(lambda peer: ret_out.at[peer], ret_in, 4)

    @pl.when(relocating)
    def _():
        wait_bytes(m_in, recv_sems.at[3])
        wide_m[...] = m_in[...].astype(F32).reshape(n * 16, hd)
        late_normed = rms_scaled(unpack(wide_m, lambda c: c, 16), gain_moe)
        ordered = jnp.dot(moves, late_normed, preferred_element_type=F32).astype(BF)
        late_result = run_expert(ordered)

        late_middle = jnp.concatenate(
            [wide_m[pl.ds(origin * 16 + c, 1), :] for c in range(cols)], axis=1
        )
        late_middle = jnp.broadcast_to(late_middle, (half, width))
        for c in range(cols):
            wide_m[pl.ds(c, n, stride=16), :] = late_result[:, c * hd : (c + 1) * hd]
        late_out[...] = wide_m[...].reshape(n, 16, hd).astype(BF)
        to_all(lambda peer: late_out.at[peer], late_in, 5)
        late_blend = in_parts(
            jnp.where(
                lane < n,
                route_weights(rms_scaled(late_middle, gain_moe), route),
                0.0,
            )[:, :n]
        )
        wait_bytes(late_in, recv_sems.at[5])
        wide_m[...] = late_in[...].astype(F32).reshape(n * 16, hd)
        late = late_middle + blended(late_blend, unpack(wide_m, lambda c: c, 16).astype(BF))
        fin[half - 1 : half, :] = late[half - 1 : half, :]

    wait_bytes(ret_in, recv_sems.at[4])
    wide_b[...] = ret_in[...].astype(F32).reshape(n * 2 * cols, hd)
    done = middle + blended(blend_parts, unpack_pair())
    kept = (lax.broadcasted_iota(jnp.int32, (half, width), 0) == half - 1) & relocating
    out_ref[...] = jnp.where(kept, fin[...], done).astype(BF)

    cross.wait_send()
    for swap in swaps:
        swap.wait_send()
    for phase, ref in ((0, q_in), (2, disp_in), (4, ret_in)):
        wait_bytes(ref.at[pl.ds(0, n - 1)], send_sems.at[phase])

    @pl.when(first_core)
    def _():
        row_copy().wait_send()

    @pl.when(relocating)
    def _():
        for phase, ref in ((1, t_in), (3, m_in), (5, late_in)):
            wait_bytes(ref.at[pl.ds(0, n - 1)], send_sems.at[phase])


def solution(mesh):
    n = mesh.shape["req"]

    def shards(
        tokens,
        gain_attn,
        w_query,
        w_key,
        w_value,
        w_out,
        cache_k,
        cache_v,
        page_table,
        lengths,
        new_owner,
        gain_moe,
        w_router,
        routes,
        w_gate,
        w_up,
        w_down,
    ):
        slots, width = tokens.shape
        half = slots // 2
        hd = w_key.shape[1]
        cols = width // hd
        experts = n // 2
        span = page_table.shape[1] * cache_k.shape[1]
        hidden = w_gate.shape[2]
        hbm = pl.BlockSpec(memory_space=pl.ANY)
        dma = pltpu.SemaphoreType.DMA
        return pl.pallas_call(
            functools.partial(layer_kernel, n),
            out_shape=pltpu.VMEM((half, width), BF),
            in_specs=[hbm] * 4 + [hbm] * 13,
            out_specs=pl.BlockSpec(memory_space=pltpu.VMEM),
            scratch_shapes=[
                pltpu.VMEM((slots, width), BF),
                pltpu.VMEM((width,), BF),
                pltpu.VMEM((width,), BF),
                pltpu.VMEM((width, w_query.shape[1] + 2 * hd), BF),
                pltpu.VMEM(w_out.shape, BF),
                pltpu.VMEM(cache_k.shape, BF),
                pltpu.VMEM(cache_v.shape, BF),
                pltpu.VMEM(w_router.shape[::-1], BF),
                pltpu.VMEM((2, hidden, width), BF),
                pltpu.VMEM((2, hidden, width), BF),
                pltpu.VMEM((2, hidden, width), BF),
                pltpu.VMEM((slots * 8, hd), F32),
                pltpu.VMEM((slots * 8, span), F32),
                pltpu.VMEM((slots * 8, hd), F32),
                pltpu.VMEM((8, hd), BF),
                pltpu.VMEM((n, 8, hd), BF),
                pltpu.VMEM((2, half, width), F32),
                pltpu.VMEM((half, width), F32),
                pltpu.VMEM((experts * 2 * cols, hd), F32),
                pltpu.VMEM((experts, 2 * cols, hd), BF),
                pltpu.VMEM((n, 2 * cols, hd), BF),
                pltpu.VMEM((n * 2 * cols, hd), F32),
                pltpu.VMEM((n, 2 * cols, hd), BF),
                pltpu.VMEM((n, 2 * cols, hd), BF),
                pltpu.SMEM(page_table.shape[::-1], jnp.int32),
                pltpu.SMEM(lengths.shape, jnp.int32),
                pltpu.SMEM(new_owner.shape, jnp.int32),
                pltpu.SMEM(routes.shape[::-1], jnp.int32),
                pltpu.VMEM((half, width), F32),
                pltpu.VMEM((1, width), F32),
                pltpu.VMEM((1, width), F32),
                pltpu.VMEM((16, hd), BF),
                pltpu.VMEM((n, 16, hd), BF),
                pltpu.VMEM((16, hd), F32),
                pltpu.VMEM((16, hd), BF),
                pltpu.VMEM((n, 16, hd), BF),
                pltpu.VMEM((n * 16, hd), F32),
                pltpu.VMEM((n, 16, hd), BF),
                pltpu.VMEM((n, 16, hd), BF),
                dma((17,)),
                dma((3,)),
                dma((3,)),
                dma,
                dma,
                dma,
                dma,
                dma((6,)),
                dma((6,)),
            ],
            compiler_params=pltpu.CompilerParams(
                collective_id=0, has_side_effects=True, vmem_limit_bytes=60 * 1024 * 1024
            ),
        )(
            page_table.T,
            lengths,
            new_owner,
            routes.T,
            tokens,
            gain_attn,
            gain_moe,
            w_query,
            w_key,
            w_value,
            w_out,
            cache_k,
            cache_v,
            w_router.T,
            jnp.swapaxes(w_gate, 1, 2),
            jnp.swapaxes(w_up, 1, 2),
            jnp.swapaxes(w_down, 1, 2),
        )

    return jax.shard_map(
        shards,
        mesh=mesh,
        in_specs=(
            P("req", None),
            P(),
            P(None, "kv"),
            P(None, "kv"),
            P(None, "kv"),
            P("kv", None),
            P("req", None, "kv"),
            P("req", None, "kv"),
            P("req", None),
            P(),
            P(),
            P(),
            P(),
            P(("req", "kv"), None),
            P("req", None, "kv"),
            P("req", None, "kv"),
            P("req", None, "kv"),
        ),
        out_specs=P(("req", "kv"), None),
        check_vma=False,
    )
```

```python
import functools
import itertools

import jax
import jax.numpy as jnp
from jax import lax
from jax.experimental import pallas as pl
from jax.experimental.pallas import tpu as pltpu
from jax.sharding import PartitionSpec as P

BF = jnp.bfloat16
F32 = jnp.float32
LAST = (((1,), (1,)), ((), ()))


def rms_scaled(wide, gain_row):
    squares = jnp.mean(wide * wide, axis=-1, keepdims=True)
    return (wide * lax.rsqrt(squares + 1e-06) * gain_row).astype(BF)


def wait_bytes(ref, sem):
    pltpu.make_async_copy(ref, ref, sem).wait()


def layer_kernel(
    n,
    pages_h,
    lengths_h,
    owner_h,
    routes_h,
    tokens_h,
    gain_a_h,
    gain_m_h,
    wq_h,
    wk_h,
    wv_h,
    wo_h,
    ck_h,
    cv_h,
    wr_h,
    wg_h,
    wu_h,
    wd_h,
    out_ref,
    tok,
    gain_a,
    gain_m,
    wqkv,
    wo,
    ck,
    cv,
    wr,
    wg,
    wu,
    wd,
    heads,
    scores,
    att,
    q_out,
    q_in,
    head_sum,
    head_in,
    wide_a,
    disp_out,
    disp_in,
    wide_b,
    ret_out,
    ret_in,
    pages_s,
    lengths_s,
    owner_s,
    routes_s,
    fin,
    row_sum,
    row_in,
    t_out,
    t_in,
    m_wide,
    m_out,
    m_in,
    wide_m,
    late_out,
    late_in,
    load_sems,
    w_send,
    w_recv,
    h_send,
    h_recv,
    r_send,
    r_recv,
    send_sems,
    recv_sems,
):
    me = lax.axis_index("req")
    kv = lax.axis_index("kv")
    slots, width = tok.shape
    half = slots // 2
    hd = ck.shape[2]
    page = ck.shape[1]
    per_slot = pages_s.shape[0]
    groups = wo.shape[0] // hd
    experts = n // 2
    cols = width // hd
    inv_root = hd ** (-0.5)

    side = round(n ** (1 / 3))
    me_z, me_x, me_y = me // (side * side), lax.rem(me // side, side), lax.rem(me, side)
    turn = 1 + (side - 2) * kv
    at_z = [lax.rem(me_z + d * turn, side) * (side * side) for d in range(side)]
    at_x = [lax.rem(me_x + d * turn, side) * side for d in range(side)]
    at_y = [lax.rem(me_y + d * turn, side) for d in range(side)]

    def hops(offset):
        return sum(min(d, side - d) for d in offset)

    offsets = sorted(
        (o for o in itertools.product(range(side), repeat=3) if any(o)), key=lambda o: -hops(o)
    )

    def shifted(offset):
        dz, dx, dy = offset
        return at_z[dz] + at_x[dx] + at_y[dy]

    sibling = {"kv": 1 - kv}
    relocating = kv == 1
    barrier = pltpu.get_barrier_semaphore()
    for offset in offsets:
        pl.semaphore_signal(barrier, 1, device_id={"req": shifted(offset)})
    pl.semaphore_signal(barrier, 1, device_id=sibling)

    def load(src, dst, i):
        copy = pltpu.make_async_copy(src, dst, load_sems.at[i])
        copy.start()
        return copy

    qcols = wq_h.shape[1]
    l_tok = load(tokens_h, tok, 0)
    l_gain = load(gain_a_h, gain_a, 1)
    l_gain_m = load(gain_m_h, gain_m, 12)
    l_wq = load(wq_h, wqkv.at[:, pl.ds(0, qcols)], 2)
    l_wk = load(wk_h, wqkv.at[:, pl.ds(qcols, hd)], 3)
    l_wv = load(wv_h, wqkv.at[:, pl.ds(qcols + hd, hd)], 4)

    l_ints = [
        load(src, dst, 13 + i)
        for i, (src, dst) in enumerate(
            (
                (pages_h, pages_s),
                (lengths_h, lengths_s),
                (owner_h, owner_s),
                (routes_h, routes_s),
            )
        )
    ]
    l_ck = load(ck_h, ck, 5)
    l_cv = load(cv_h, cv, 6)
    l_wo = load(wo_h, wo, 7)
    l_wr = load(wr_h, wr, 8)
    l_wg = load(wg_h.at[0], wg.at[0], 9)
    l_wu = load(wu_h.at[0], wu.at[0], 10)
    l_wd = load(wd_h.at[0], wd.at[0], 11)

    def to_all(src_of, dst, phase):
        for offset in offsets:
            peer = shifted(offset)
            pltpu.make_async_remote_copy(
                src_ref=src_of(peer),
                dst_ref=dst.at[me],
                send_sem=send_sems.at[phase],
                recv_sem=recv_sems.at[phase],
                device_id={"req": peer},
            ).start()
        pltpu.make_async_copy(src_of(me), dst.at[me], recv_sems.at[phase]).start()

    l_tok.wait()
    l_gain.wait()
    l_gain_m.wait()
    gain_attn = gain_a[...].astype(F32).reshape(1, width)
    gain_moe = gain_m[...].astype(F32).reshape(1, width)
    tokf = tok[...].astype(F32)
    normed = rms_scaled(tokf, gain_attn)
    last = (slots - 1) * 8
    m_wide[...] = jnp.zeros((16, hd), F32)
    for c in range(cols):
        m_wide[c : c + 1, :] = tokf[slots - 1 : slots, c * hd : (c + 1) * hd]
    t_out[...] = m_wide[...].astype(BF)
    l_wq.wait()
    l_wk.wait()
    l_wv.wait()
    qkv = jnp.dot(normed, wqkv[...], preferred_element_type=F32).astype(BF).astype(F32)
    for h in range(groups + 2):
        heads[pl.ds(h, slots, stride=8), :] = qkv[:, h * hd : (h + 1) * hd]
    q_out[...] = heads[last : last + 8, :].astype(BF)
    pl.semaphore_wait(barrier, n)
    to_all(lambda peer: q_out, q_in, 0)

    @pl.when(relocating)
    def _():
        to_all(lambda peer: t_out, t_in, 1)

    def attend(first, count):
        rows = slice(first * 8, (first + count) * 8)
        place = lax.broadcasted_iota(jnp.int32, (8, page), 1)
        for s in range(first, first + count):
            block = heads[s * 8 : s * 8 + 8, :].astype(BF)
            live = lengths_s[me * slots + s]
            for j in range(per_slot):
                dots = lax.dot_general(
                    block, ck[pages_s[j, s]], LAST, preferred_element_type=F32
                )
                scores[s * 8 : s * 8 + 8, j * page : (j + 1) * page] = jnp.where(
                    place + j * page < live, dots * inv_root, -1e30
                )
        all_scores = scores[rows, :]
        top = jnp.max(all_scores, axis=-1, keepdims=True)
        weights = jnp.exp(all_scores - top)
        total = jnp.sum(weights, axis=-1, keepdims=True)
        scores[rows, :] = weights
        for s in range(first, first + count):
            acc = jnp.zeros((8, hd), F32)
            for j in range(per_slot):
                acc = acc + jnp.dot(
                    scores[s * 8 : s * 8 + 8, j * page : (j + 1) * page].astype(BF),
                    cv[pages_s[j, s]],
                    preferred_element_type=F32,
                )
            att[s * 8 : s * 8 + 8, :] = acc
        block = heads[rows, :].reshape(count, 8, hd)
        own = jnp.sum(block * block[:, groups : groups + 1, :], axis=-1, keepdims=True) * inv_root
        top = top.reshape(count, 8, 1)
        total = total.reshape(count, 8, 1)
        joint = jnp.maximum(top, own)
        old_part = jnp.exp(top - joint)
        new_part = jnp.exp(own - joint)
        merged = (
            att[rows, :].reshape(count, 8, hd) * old_part
            + new_part * block[:, groups + 1 : groups + 2, :]
        )
        result = merged / (total * old_part + new_part)
        att[rows, :] = result.astype(BF).astype(F32).reshape(count * 8, hd)

    for l_int in l_ints:
        l_int.wait()
    l_ck.wait()
    l_cv.wait()
    attend(0, slots - 1)
    att[last : last + 8, :] = jnp.zeros((8, hd), F32)
    l_wo.wait()

    def head_terms():
        attended = jnp.concatenate(
            [att[pl.ds(h, slots, stride=8), :].astype(BF) for h in range(groups)], axis=1
        )
        return jnp.dot(attended, wo[...], preferred_element_type=F32)

    terms = head_terms()
    head_sum[0] = terms[:half]
    head_sum[1] = terms[half:]
    cross = pltpu.make_async_remote_copy(
        src_ref=head_sum.at[1 - kv],
        dst_ref=head_in,
        send_sem=h_send,
        recv_sem=h_recv,
        device_id=sibling,
    )
    cross.start()
    first_core = kv == 0
    mine = jnp.where(first_core, terms[:half], terms[half:])
    residual = jnp.where(first_core, tokf[:half], tokf[half:])

    topk = routes_s.shape[0]
    lane = lax.broadcasted_iota(jnp.int32, (half, 128), 1)
    row = lax.broadcasted_iota(jnp.int32, (half, 128), 0)
    late_row = (row == half - 1) & relocating
    route = []
    for j in range(topk):
        named_by = jnp.zeros((half, 128), jnp.int32)
        for i in range(half):
            named_by = jnp.where(row == i, routes_s[j, i], named_by)
        route.append(named_by)
    early = [jnp.where(late_row, -1, r) for r in route]

    def places(expert, slot):
        named = jnp.zeros((half, 128), F32)
        for j in range(topk):
            named = named + jnp.where(early[j] == expert, 1.0, 0.0)
        rank = jnp.zeros((half, 128), F32)
        for i in range(half - 1):
            rank = rank + jnp.where(row > i, named[i : i + 1, :], 0.0)
        return jnp.where(rank == slot.astype(F32), named, 0.0)

    pick = places(lane % experts, lane // experts)
    pick_t = jnp.transpose(pick)[: 2 * experts, :].astype(BF)
    peer_expert = (lane % n) // 2
    peer_place = places(peer_expert, lane // n)

    cross.wait_recv()
    middle = (residual + (mine + head_in[...])).astype(BF).astype(F32)
    normed_two = rms_scaled(middle, gain_moe)
    outgoing = jnp.dot(pick_t, normed_two, preferred_element_type=F32)
    for c in range(cols):
        for k in range(2):
            wide_a[pl.ds(c * 2 + k, experts, stride=2 * cols), :] = outgoing[
                k * experts : (k + 1) * experts, c * hd : (c + 1) * hd
            ]
    disp_out[...] = wide_a[...].reshape(experts, 2 * cols, hd).astype(BF)
    to_all(lambda peer: disp_out.at[peer // 2], disp_in, 2)
    swaps = []
    for i, (src, dst) in enumerate(((wg_h, wg), (wu_h, wu), (wd_h, wd))):
        swap = pltpu.make_async_remote_copy(
            src_ref=src.at[0],
            dst_ref=dst.at[1],
            send_sem=w_send.at[i],
            recv_sem=w_recv.at[i],
            device_id=sibling,
        )
        swap.start()
        swaps.append(swap)

    wait_bytes(q_in, recv_sems.at[0])
    served = owner_s[me]
    heads[last : last + 8, :] = q_in[served].astype(F32)
    attend(slots - 1, 1)
    late_terms = head_terms()[slots - 1 : slots, :]
    row_sum[...] = late_terms

    def row_copy():
        return pltpu.make_async_remote_copy(
            src_ref=row_sum,
            dst_ref=row_in,
            send_sem=r_send,
            recv_sem=r_recv,
            device_id=sibling,
        )

    @pl.when(first_core)
    def _():
        row_copy().start()

    l_wr.wait()

    def route_weights(normed_rows, chosen_by):
        logits = lax.dot_general(normed_rows, wr[...], LAST, preferred_element_type=F32)
        choice = lax.broadcasted_iota(jnp.int32, logits.shape, 1)
        chosen = [
            jnp.sum(jnp.where(choice == r[:, :experts], logits, 0.0), axis=-1, keepdims=True)
            for r in chosen_by
        ]
        best = functools.reduce(jnp.maximum, chosen)
        powers = [jnp.exp(c - best) for c in chosen]
        denom = functools.reduce(jnp.add, powers)
        blend = jnp.zeros((half, 128), F32)
        for r, power in zip(chosen_by, powers):
            blend = blend + jnp.where(r == peer_expert, power / denom, 0.0)
        return blend

    def in_parts(blend):
        part_a = blend.astype(BF).astype(F32)
        part_b = (blend - part_a).astype(BF).astype(F32)
        part_c = blend - part_a - part_b
        return jnp.concatenate([part_a, part_b, part_c], axis=0).astype(BF)

    def blended(parts, rows):
        mixed = jnp.dot(parts, rows, preferred_element_type=F32)
        return mixed[:half] + mixed[half : 2 * half] + mixed[2 * half :]

    blend_parts = in_parts(route_weights(normed_two, early) * peer_place)

    @pl.when(relocating)
    def _():
        wait_bytes(t_in, recv_sems.at[1])
        row_copy().wait_recv()
        total = row_sum[...] + row_in[...]
        for c in range(cols):
            m_wide[c : c + 1, :] = total[:, c * hd : (c + 1) * hd]
        m_out[...] = (t_in[served].astype(F32) + m_wide[...]).astype(BF)
        to_all(lambda peer: m_out, m_in, 3)

    def run_expert(rows):
        result = None
        for t in range(2):
            gate = lax.dot_general(rows, wg[t], LAST, preferred_element_type=F32)
            up = lax.dot_general(rows, wu[t], LAST, preferred_element_type=F32)
            hidden = (jnp.maximum(gate, 0.0) * up).astype(BF)
            part = jnp.dot(hidden, wd[t], preferred_element_type=F32)
            result = part if result is None else result + part
        return result

    def unpack(wide, first, stride):
        return jnp.concatenate(
            [wide[pl.ds(first(c), n, stride=stride), :] for c in range(cols)], axis=1
        )

    def unpack_pair():
        return jnp.concatenate(
            [unpack(wide_b, lambda c: c * 2 + k, 2 * cols).astype(BF) for k in range(2)], axis=0
        )

    owners = jnp.zeros((8, 128), jnp.int32)
    owner_lane = lax.broadcasted_iota(jnp.int32, (8, 128), 1)
    for c in range(n):
        owners = jnp.where(owner_lane == c, owner_s[c], owners)
    slot_row = lax.broadcasted_iota(jnp.int32, (n, n), 0)
    moves = jnp.where(slot_row == owners[0:1, :n], 1.0, 0.0).astype(BF)

    def find(c, found):
        return jnp.where(owner_s[c] == me, c, found)

    origin = lax.fori_loop(0, n, find, 0)
    l_wg.wait()
    l_wu.wait()
    l_wd.wait()
    for swap in swaps:
        swap.wait_recv()
    wait_bytes(disp_in, recv_sems.at[2])
    wide_b[...] = disp_in[...].astype(F32).reshape(n * 2 * cols, hd)
    result = run_expert(unpack_pair())
    for c in range(cols):
        for k in range(2):
            wide_b[pl.ds(c * 2 + k, n, stride=2 * cols), :] = result[
                k * n : (k + 1) * n, c * hd : (c + 1) * hd
            ]
    ret_out[...] = wide_b[...].reshape(n, 2 * cols, hd).astype(BF)
    to_all(lambda peer: ret_out.at[peer], ret_in, 4)

    @pl.when(relocating)
    def _():
        wait_bytes(m_in, recv_sems.at[3])
        wide_m[...] = m_in[...].astype(F32).reshape(n * 16, hd)
        late_normed = rms_scaled(unpack(wide_m, lambda c: c, 16), gain_moe)
        ordered = jnp.dot(moves, late_normed, preferred_element_type=F32).astype(BF)
        late_result = run_expert(ordered)

        late_middle = jnp.concatenate(
            [wide_m[pl.ds(origin * 16 + c, 1), :] for c in range(cols)], axis=1
        )
        late_middle = jnp.broadcast_to(late_middle, (half, width))
        for c in range(cols):
            wide_m[pl.ds(c, n, stride=16), :] = late_result[:, c * hd : (c + 1) * hd]
        late_out[...] = wide_m[...].reshape(n, 16, hd).astype(BF)
        to_all(lambda peer: late_out.at[peer], late_in, 5)
        late_blend = in_parts(
            jnp.where(
                lane < n,
                route_weights(rms_scaled(late_middle, gain_moe), route),
                0.0,
            )[:, :n]
        )
        wait_bytes(late_in, recv_sems.at[5])
        wide_m[...] = late_in[...].astype(F32).reshape(n * 16, hd)
        late = late_middle + blended(late_blend, unpack(wide_m, lambda c: c, 16).astype(BF))
        fin[half - 1 : half, :] = late[half - 1 : half, :]

    wait_bytes(ret_in, recv_sems.at[4])
    wide_b[...] = ret_in[...].astype(F32).reshape(n * 2 * cols, hd)
    done = middle + blended(blend_parts, unpack_pair())
    kept = (lax.broadcasted_iota(jnp.int32, (half, width), 0) == half - 1) & relocating
    out_ref[...] = jnp.where(kept, fin[...], done).astype(BF)

    cross.wait_send()
    for swap in swaps:
        swap.wait_send()
    for phase, ref in ((0, q_in), (2, disp_in), (4, ret_in)):
        wait_bytes(ref.at[pl.ds(0, n - 1)], send_sems.at[phase])

    @pl.when(first_core)
    def _():
        row_copy().wait_send()

    @pl.when(relocating)
    def _():
        for phase, ref in ((1, t_in), (3, m_in), (5, late_in)):
            wait_bytes(ref.at[pl.ds(0, n - 1)], send_sems.at[phase])


def solution(mesh):
    n = mesh.shape["req"]

    def shards(
        tokens,
        gain_attn,
        w_query,
        w_key,
        w_value,
        w_out,
        cache_k,
        cache_v,
        page_table,
        lengths,
        new_owner,
        gain_moe,
        w_router,
        routes,
        w_gate,
        w_up,
        w_down,
    ):
        slots, width = tokens.shape
        half = slots // 2
        hd = w_key.shape[1]
        cols = width // hd
        experts = n // 2
        span = page_table.shape[1] * cache_k.shape[1]
        hidden = w_gate.shape[2]
        hbm = pl.BlockSpec(memory_space=pl.ANY)
        dma = pltpu.SemaphoreType.DMA
        return pl.pallas_call(
            functools.partial(layer_kernel, n),
            out_shape=pltpu.VMEM((half, width), BF),
            in_specs=[hbm] * 4 + [hbm] * 13,
            out_specs=pl.BlockSpec(memory_space=pltpu.VMEM),
            scratch_shapes=[
                pltpu.VMEM((slots, width), BF),
                pltpu.VMEM((width,), BF),
                pltpu.VMEM((width,), BF),
                pltpu.VMEM((width, w_query.shape[1] + 2 * hd), BF),
                pltpu.VMEM(w_out.shape, BF),
                pltpu.VMEM(cache_k.shape, BF),
                pltpu.VMEM(cache_v.shape, BF),
                pltpu.VMEM(w_router.shape[::-1], BF),
                pltpu.VMEM((2, hidden, width), BF),
                pltpu.VMEM((2, hidden, width), BF),
                pltpu.VMEM((2, hidden, width), BF),
                pltpu.VMEM((slots * 8, hd), F32),
                pltpu.VMEM((slots * 8, span), F32),
                pltpu.VMEM((slots * 8, hd), F32),
                pltpu.VMEM((8, hd), BF),
                pltpu.VMEM((n, 8, hd), BF),
                pltpu.VMEM((2, half, width), F32),
                pltpu.VMEM((half, width), F32),
                pltpu.VMEM((experts * 2 * cols, hd), F32),
                pltpu.VMEM((experts, 2 * cols, hd), BF),
                pltpu.VMEM((n, 2 * cols, hd), BF),
                pltpu.VMEM((n * 2 * cols, hd), F32),
                pltpu.VMEM((n, 2 * cols, hd), BF),
                pltpu.VMEM((n, 2 * cols, hd), BF),
                pltpu.SMEM(page_table.shape[::-1], jnp.int32),
                pltpu.SMEM(lengths.shape, jnp.int32),
                pltpu.SMEM(new_owner.shape, jnp.int32),
                pltpu.SMEM(routes.shape[::-1], jnp.int32),
                pltpu.VMEM((half, width), F32),
                pltpu.VMEM((1, width), F32),
                pltpu.VMEM((1, width), F32),
                pltpu.VMEM((16, hd), BF),
                pltpu.VMEM((n, 16, hd), BF),
                pltpu.VMEM((16, hd), F32),
                pltpu.VMEM((16, hd), BF),
                pltpu.VMEM((n, 16, hd), BF),
                pltpu.VMEM((n * 16, hd), F32),
                pltpu.VMEM((n, 16, hd), BF),
                pltpu.VMEM((n, 16, hd), BF),
                dma((17,)),
                dma((3,)),
                dma((3,)),
                dma,
                dma,
                dma,
                dma,
                dma((6,)),
                dma((6,)),
            ],
            compiler_params=pltpu.CompilerParams(
                collective_id=0, has_side_effects=True, vmem_limit_bytes=60 * 1024 * 1024
            ),
        )(
            page_table.T,
            lengths,
            new_owner,
            routes.T,
            tokens,
            gain_attn,
            gain_moe,
            w_query,
            w_key,
            w_value,
            w_out,
            cache_k,
            cache_v,
            w_router.T,
            jnp.swapaxes(w_gate, 1, 2),
            jnp.swapaxes(w_up, 1, 2),
            jnp.swapaxes(w_down, 1, 2),
        )

    return jax.shard_map(
        shards,
        mesh=mesh,
        in_specs=(
            P("req", None),
            P(),
            P(None, "kv"),
            P(None, "kv"),
            P(None, "kv"),
            P("kv", None),
            P("req", None, "kv"),
            P("req", None, "kv"),
            P("req", None),
            P(),
            P(),
            P(),
            P(),
            P(("req", "kv"), None),
            P("req", None, "kv"),
            P("req", None, "kv"),
            P("req", None, "kv"),
        ),
        out_specs=P(("req", "kv"), None),
        check_vma=False,
    )
```

```python
import functools
import itertools

import jax
import jax.numpy as jnp
from jax import lax
from jax.experimental import pallas as pl
from jax.experimental.pallas import tpu as pltpu
from jax.sharding import PartitionSpec as P

BF = jnp.bfloat16
F32 = jnp.float32
LAST = (((1,), (1,)), ((), ()))


def rms_scaled(wide, gain_row):
    squares = jnp.mean(wide * wide, axis=-1, keepdims=True)
    return (wide * lax.rsqrt(squares + 1e-06) * gain_row).astype(BF)


def wait_bytes(ref, sem):
    pltpu.make_async_copy(ref, ref, sem).wait()


def layer_kernel(
    n,
    pages_h,
    lengths_h,
    owner_h,
    routes_h,
    tokens_h,
    gain_a_h,
    gain_m_h,
    wq_h,
    wk_h,
    wv_h,
    wo_h,
    ck_h,
    cv_h,
    wr_h,
    wg_h,
    wu_h,
    wd_h,
    out_ref,
    tok,
    gain_a,
    gain_m,
    wqkv,
    wo,
    ck,
    cv,
    wr,
    wg,
    wu,
    wd,
    heads,
    scores,
    att,
    q_out,
    q_in,
    head_sum,
    head_in,
    wide_a,
    disp_out,
    disp_in,
    wide_b,
    ret_out,
    ret_in,
    pages_s,
    lengths_s,
    owner_s,
    routes_s,
    mid_late,
    early_mix,
    late_mix,
    row_sum,
    row_in,
    t_out,
    t_in,
    m_wide,
    m_out,
    m_in,
    wide_m,
    late_out,
    late_in,
    load_sems,
    w_send,
    w_recv,
    h_send,
    h_recv,
    r_send,
    r_recv,
    send_sems,
    recv_sems,
):
    me = lax.axis_index("req")
    kv = lax.axis_index("kv")
    slots, width = tok.shape
    half = slots // 2
    hd = ck.shape[2]
    page = ck.shape[1]
    per_slot = pages_s.shape[0]
    groups = wo.shape[0] // hd
    experts = n // 2
    cols = width // hd
    inv_root = hd ** (-0.5)

    side = round(n ** (1 / 3))
    me_z, me_x, me_y = me // (side * side), lax.rem(me // side, side), lax.rem(me, side)
    turn = 1 + (side - 2) * kv
    at_z = [lax.rem(me_z + d * turn, side) * (side * side) for d in range(side)]
    at_x = [lax.rem(me_x + d * turn, side) * side for d in range(side)]
    at_y = [lax.rem(me_y + d * turn, side) for d in range(side)]

    def hops(offset):
        return sum(min(d, side - d) for d in offset)

    offsets = sorted(
        (o for o in itertools.product(range(side), repeat=3) if any(o)), key=lambda o: -hops(o)
    )

    def shifted(offset):
        dz, dx, dy = offset
        return at_z[dz] + at_x[dx] + at_y[dy]

    sibling = {"kv": 1 - kv}
    relocating = kv == 1
    barrier = pltpu.get_barrier_semaphore()
    for offset in offsets:
        pl.semaphore_signal(barrier, 1, device_id={"req": shifted(offset)})
    pl.semaphore_signal(barrier, 1, device_id=sibling)

    def load(src, dst, i):
        copy = pltpu.make_async_copy(src, dst, load_sems.at[i])
        copy.start()
        return copy

    qcols = wq_h.shape[1]
    l_tok = load(tokens_h, tok, 0)
    l_gain = load(gain_a_h, gain_a, 1)
    l_gain_m = load(gain_m_h, gain_m, 12)
    l_wq = load(wq_h, wqkv.at[:, pl.ds(0, qcols)], 2)
    l_wk = load(wk_h, wqkv.at[:, pl.ds(qcols, hd)], 3)
    l_wv = load(wv_h, wqkv.at[:, pl.ds(qcols + hd, hd)], 4)

    l_ints = [
        load(src, dst, 13 + i)
        for i, (src, dst) in enumerate(
            (
                (pages_h, pages_s),
                (lengths_h, lengths_s),
                (owner_h, owner_s),
                (routes_h, routes_s),
            )
        )
    ]
    l_ck = load(ck_h, ck, 5)
    l_cv = load(cv_h, cv, 6)
    l_wo = load(wo_h, wo, 7)
    l_wr = load(wr_h, wr, 8)
    l_wg = load(wg_h.at[0], wg.at[0], 9)
    l_wu = load(wu_h.at[0], wu.at[0], 10)
    l_wd = load(wd_h.at[0], wd.at[0], 11)

    def to_all(src_of, dst, phase):
        for offset in offsets:
            peer = shifted(offset)
            pltpu.make_async_remote_copy(
                src_ref=src_of(peer),
                dst_ref=dst.at[me],
                send_sem=send_sems.at[phase],
                recv_sem=recv_sems.at[phase],
                device_id={"req": peer},
            ).start()
        pltpu.make_async_copy(src_of(me), dst.at[me], recv_sems.at[phase]).start()

    l_tok.wait()
    l_gain.wait()
    l_gain_m.wait()
    gain_attn = gain_a[...].astype(F32).reshape(1, width)
    gain_moe = gain_m[...].astype(F32).reshape(1, width)
    tokf = tok[...].astype(F32)
    normed = rms_scaled(tokf, gain_attn)
    last = (slots - 1) * 8
    m_wide[...] = jnp.zeros((16, hd), F32)
    for c in range(cols):
        m_wide[c : c + 1, :] = tokf[slots - 1 : slots, c * hd : (c + 1) * hd]
    t_out[...] = m_wide[...].astype(BF)
    l_wq.wait()
    l_wk.wait()
    l_wv.wait()
    qkv = jnp.dot(normed, wqkv[...], preferred_element_type=F32).astype(BF).astype(F32)
    for h in range(groups + 2):
        heads[pl.ds(h, slots, stride=8), :] = qkv[:, h * hd : (h + 1) * hd]
    q_out[...] = heads[last : last + 8, :].astype(BF)
    pl.semaphore_wait(barrier, n)
    to_all(lambda peer: q_out, q_in, 0)

    @pl.when(relocating)
    def _():
        to_all(lambda peer: t_out, t_in, 1)

    def attend(first, count):
        rows = slice(first * 8, (first + count) * 8)
        place = lax.broadcasted_iota(jnp.int32, (8, page), 1)
        for s in range(first, first + count):
            block = heads[s * 8 : s * 8 + 8, :].astype(BF)
            live = lengths_s[me * slots + s]
            for j in range(per_slot):
                dots = lax.dot_general(
                    block, ck[pages_s[j, s]], LAST, preferred_element_type=F32
                )
                scores[s * 8 : s * 8 + 8, j * page : (j + 1) * page] = jnp.where(
                    place + j * page < live, dots * inv_root, -1e30
                )
        all_scores = scores[rows, :]
        top = jnp.max(all_scores, axis=-1, keepdims=True)
        weights = jnp.exp(all_scores - top)
        total = jnp.sum(weights, axis=-1, keepdims=True)
        scores[rows, :] = weights
        for s in range(first, first + count):
            acc = jnp.zeros((8, hd), F32)
            for j in range(per_slot):
                acc = acc + jnp.dot(
                    scores[s * 8 : s * 8 + 8, j * page : (j + 1) * page].astype(BF),
                    cv[pages_s[j, s]],
                    preferred_element_type=F32,
                )
            att[s * 8 : s * 8 + 8, :] = acc
        block = heads[rows, :].reshape(count, 8, hd)
        own = jnp.sum(block * block[:, groups : groups + 1, :], axis=-1, keepdims=True) * inv_root
        top = top.reshape(count, 8, 1)
        total = total.reshape(count, 8, 1)
        joint = jnp.maximum(top, own)
        old_part = jnp.exp(top - joint)
        new_part = jnp.exp(own - joint)
        merged = (
            att[rows, :].reshape(count, 8, hd) * old_part
            + new_part * block[:, groups + 1 : groups + 2, :]
        )
        result = merged / (total * old_part + new_part)
        att[rows, :] = result.astype(BF).astype(F32).reshape(count * 8, hd)

    for l_int in l_ints:
        l_int.wait()
    l_ck.wait()
    l_cv.wait()
    attend(0, slots - 1)
    att[last : last + 8, :] = jnp.zeros((8, hd), F32)
    l_wo.wait()

    def head_terms():
        attended = jnp.concatenate(
            [att[pl.ds(h, slots, stride=8), :].astype(BF) for h in range(groups)], axis=1
        )
        return jnp.dot(attended, wo[...], preferred_element_type=F32)

    terms = head_terms()
    head_sum[0] = terms[:half]
    head_sum[1] = terms[half:]
    cross = pltpu.make_async_remote_copy(
        src_ref=head_sum.at[1 - kv],
        dst_ref=head_in,
        send_sem=h_send,
        recv_sem=h_recv,
        device_id=sibling,
    )
    cross.start()
    first_core = kv == 0
    mine = jnp.where(first_core, terms[:half], terms[half:])
    residual = jnp.where(first_core, tokf[:half], tokf[half:])

    topk = routes_s.shape[0]
    lane = lax.broadcasted_iota(jnp.int32, (half, 128), 1)
    row = lax.broadcasted_iota(jnp.int32, (half, 128), 0)
    late_row = (row == half - 1) & relocating
    route = []
    for j in range(topk):
        named_by = jnp.zeros((half, 128), jnp.int32)
        for i in range(half):
            named_by = jnp.where(row == i, routes_s[j, i], named_by)
        route.append(named_by)
    early = [jnp.where(late_row, -1, r) for r in route]

    def places(expert, slot):
        named = jnp.zeros((half, 128), F32)
        for j in range(topk):
            named = named + jnp.where(early[j] == expert, 1.0, 0.0)
        rank = jnp.zeros((half, 128), F32)
        for i in range(half - 1):
            rank = rank + jnp.where(row > i, named[i : i + 1, :], 0.0)
        return jnp.where(rank == slot.astype(F32), named, 0.0)

    pick = places(lane % experts, lane // experts)
    pick_t = jnp.transpose(pick)[: 2 * experts, :].astype(BF)
    peer_expert = (lane % n) // 2
    peer_place = places(peer_expert, lane // n)

    cross.wait_recv()
    middle = (residual + (mine + head_in[...])).astype(BF).astype(F32)
    normed_two = rms_scaled(middle, gain_moe)
    outgoing = jnp.dot(pick_t, normed_two, preferred_element_type=F32)
    for c in range(cols):
        for k in range(2):
            wide_a[pl.ds(c * 2 + k, experts, stride=2 * cols), :] = outgoing[
                k * experts : (k + 1) * experts, c * hd : (c + 1) * hd
            ]
    disp_out[...] = wide_a[...].reshape(experts, 2 * cols, hd).astype(BF)
    to_all(lambda peer: disp_out.at[peer // 2], disp_in, 2)
    swaps = []
    for i, (src, dst) in enumerate(((wg_h, wg), (wu_h, wu), (wd_h, wd))):
        swap = pltpu.make_async_remote_copy(
            src_ref=src.at[0],
            dst_ref=dst.at[1],
            send_sem=w_send.at[i],
            recv_sem=w_recv.at[i],
            device_id=sibling,
        )
        swap.start()
        swaps.append(swap)

    wait_bytes(q_in, recv_sems.at[0])
    served = owner_s[me]
    heads[last : last + 8, :] = q_in[served].astype(F32)
    attend(slots - 1, 1)
    late_terms = head_terms()[slots - 1 : slots, :]
    row_sum[...] = late_terms

    def row_copy():
        return pltpu.make_async_remote_copy(
            src_ref=row_sum,
            dst_ref=row_in,
            send_sem=r_send,
            recv_sem=r_recv,
            device_id=sibling,
        )

    @pl.when(first_core)
    def _():
        row_copy().start()

    l_wr.wait()

    def route_weights(normed_rows, chosen_by):
        logits = lax.dot_general(normed_rows, wr[...], LAST, preferred_element_type=F32)
        choice = lax.broadcasted_iota(jnp.int32, logits.shape, 1)
        chosen = [
            jnp.sum(jnp.where(choice == r[:, :experts], logits, 0.0), axis=-1, keepdims=True)
            for r in chosen_by
        ]
        best = functools.reduce(jnp.maximum, chosen)
        powers = [jnp.exp(c - best) for c in chosen]
        denom = functools.reduce(jnp.add, powers)
        blend = jnp.zeros((half, 128), F32)
        for r, power in zip(chosen_by, powers):
            blend = blend + jnp.where(r == peer_expert, power / denom, 0.0)
        return blend

    def in_parts(blend):
        part_a = blend.astype(BF).astype(F32)
        part_b = (blend - part_a).astype(BF).astype(F32)
        part_c = blend - part_a - part_b
        return jnp.concatenate([part_a, part_b, part_c], axis=0).astype(BF)

    blend_parts = in_parts(route_weights(normed_two, early) * peer_place)

    def spread(parts, mix, block):
        count = parts.shape[0]
        span = n * block
        at = lax.broadcasted_iota(jnp.int32, (1, span), 1)
        owner_of = (at * (65536 // block + 1)) // 65536
        within = at - owner_of * block
        per_col = block // cols
        wanted = owner_of + (within % per_col) * n
        pick_lane = lax.broadcasted_iota(jnp.int32, (parts.shape[1], span), 0) == wanted
        wide = jnp.dot(
            parts, jnp.where(pick_lane, 1.0, 0.0).astype(BF), preferred_element_type=F32
        )
        for c in range(cols):
            mix[c * count : (c + 1) * count, :] = jnp.where(
                within // per_col == c, wide, 0.0
            ).astype(BF)

    def gathered(mix, arrived_rows):
        block = arrived_rows.shape[1]
        flat = arrived_rows[...].astype(F32).reshape(n * block, hd).astype(BF)
        sums = jnp.dot(mix[...], flat, preferred_element_type=F32)
        thirds = [sums[i * half : (i + 1) * half] for i in range(3 * cols)]
        return jnp.concatenate(
            [thirds[3 * c] + thirds[3 * c + 1] + thirds[3 * c + 2] for c in range(cols)], axis=1
        )

    @pl.when(relocating)
    def _():
        wait_bytes(t_in, recv_sems.at[1])
        row_copy().wait_recv()
        total = row_sum[...] + row_in[...]
        for c in range(cols):
            m_wide[c : c + 1, :] = total[:, c * hd : (c + 1) * hd]
        m_out[...] = (t_in[served].astype(F32) + m_wide[...]).astype(BF)
        to_all(lambda peer: m_out, m_in, 3)

    def run_expert(rows):
        result = None
        for t in range(2):
            gate = lax.dot_general(rows, wg[t], LAST, preferred_element_type=F32)
            up = lax.dot_general(rows, wu[t], LAST, preferred_element_type=F32)
            hidden = (jnp.maximum(gate, 0.0) * up).astype(BF)
            part = jnp.dot(hidden, wd[t], preferred_element_type=F32)
            result = part if result is None else result + part
        return result

    def unpack(wide, first, stride):
        return jnp.concatenate(
            [wide[pl.ds(first(c), n, stride=stride), :] for c in range(cols)], axis=1
        )

    def unpack_pair():
        return jnp.concatenate(
            [unpack(wide_b, lambda c: c * 2 + k, 2 * cols).astype(BF) for k in range(2)], axis=0
        )

    owners = jnp.zeros((8, 128), jnp.int32)
    owner_lane = lax.broadcasted_iota(jnp.int32, (8, 128), 1)
    for c in range(n):
        owners = jnp.where(owner_lane == c, owner_s[c], owners)
    slot_row = lax.broadcasted_iota(jnp.int32, (n, n), 0)
    moves = jnp.where(slot_row == owners[0:1, :n], 1.0, 0.0).astype(BF)

    def find(c, found):
        return jnp.where(owner_s[c] == me, c, found)

    origin = lax.fori_loop(0, n, find, 0)
    spread(blend_parts, early_mix, 2 * cols)
    l_wg.wait()
    l_wu.wait()
    l_wd.wait()
    for swap in swaps:
        swap.wait_recv()
    wait_bytes(disp_in, recv_sems.at[2])
    wide_b[...] = disp_in[...].astype(F32).reshape(n * 2 * cols, hd)
    result = run_expert(unpack_pair())
    for c in range(cols):
        for k in range(2):
            wide_b[pl.ds(c * 2 + k, n, stride=2 * cols), :] = result[
                k * n : (k + 1) * n, c * hd : (c + 1) * hd
            ]
    ret_out[...] = wide_b[...].reshape(n, 2 * cols, hd).astype(BF)
    to_all(lambda peer: ret_out.at[peer], ret_in, 4)

    @pl.when(relocating)
    def _():
        wait_bytes(m_in, recv_sems.at[3])
        wide_m[...] = m_in[...].astype(F32).reshape(n * 16, hd)
        late_normed = rms_scaled(unpack(wide_m, lambda c: c, 16), gain_moe)
        ordered = jnp.dot(moves, late_normed, preferred_element_type=F32).astype(BF)
        late_result = run_expert(ordered)

        late_middle = jnp.concatenate(
            [wide_m[pl.ds(origin * 16 + c, 1), :] for c in range(cols)], axis=1
        )
        late_middle = jnp.broadcast_to(late_middle, (half, width))
        for c in range(cols):
            wide_m[pl.ds(c, n, stride=16), :] = late_result[:, c * hd : (c + 1) * hd]
        late_out[...] = wide_m[...].reshape(n, 16, hd).astype(BF)
        to_all(lambda peer: late_out.at[peer], late_in, 5)
        late_blend = in_parts(
            jnp.where(
                lane < n,
                route_weights(rms_scaled(late_middle, gain_moe), route),
                0.0,
            )[:, :n]
        )
        mid_late[...] = late_middle
        spread(late_blend, late_mix, 16)

    @pl.when(relocating)
    def _():
        wait_bytes(late_in, recv_sems.at[5])

    wait_bytes(ret_in, recv_sems.at[4])
    done = middle + gathered(early_mix, ret_in)
    late = mid_late[...] + gathered(late_mix, late_in)
    kept = (lax.broadcasted_iota(jnp.int32, (half, width), 0) == half - 1) & relocating
    out_ref[...] = jnp.where(kept, late, done).astype(BF)

    cross.wait_send()
    for swap in swaps:
        swap.wait_send()
    for phase, ref in ((0, q_in), (2, disp_in), (4, ret_in)):
        wait_bytes(ref.at[pl.ds(0, n - 1)], send_sems.at[phase])

    @pl.when(first_core)
    def _():
        row_copy().wait_send()

    @pl.when(relocating)
    def _():
        for phase, ref in ((1, t_in), (3, m_in), (5, late_in)):
            wait_bytes(ref.at[pl.ds(0, n - 1)], send_sems.at[phase])


def solution(mesh):
    n = mesh.shape["req"]

    def shards(
        tokens,
        gain_attn,
        w_query,
        w_key,
        w_value,
        w_out,
        cache_k,
        cache_v,
        page_table,
        lengths,
        new_owner,
        gain_moe,
        w_router,
        routes,
        w_gate,
        w_up,
        w_down,
    ):
        slots, width = tokens.shape
        half = slots // 2
        hd = w_key.shape[1]
        cols = width // hd
        experts = n // 2
        span = page_table.shape[1] * cache_k.shape[1]
        hidden = w_gate.shape[2]
        hbm = pl.BlockSpec(memory_space=pl.ANY)
        dma = pltpu.SemaphoreType.DMA
        return pl.pallas_call(
            functools.partial(layer_kernel, n),
            out_shape=pltpu.VMEM((half, width), BF),
            in_specs=[hbm] * 4 + [hbm] * 13,
            out_specs=pl.BlockSpec(memory_space=pltpu.VMEM),
            scratch_shapes=[
                pltpu.VMEM((slots, width), BF),
                pltpu.VMEM((width,), BF),
                pltpu.VMEM((width,), BF),
                pltpu.VMEM((width, w_query.shape[1] + 2 * hd), BF),
                pltpu.VMEM(w_out.shape, BF),
                pltpu.VMEM(cache_k.shape, BF),
                pltpu.VMEM(cache_v.shape, BF),
                pltpu.VMEM(w_router.shape[::-1], BF),
                pltpu.VMEM((2, hidden, width), BF),
                pltpu.VMEM((2, hidden, width), BF),
                pltpu.VMEM((2, hidden, width), BF),
                pltpu.VMEM((slots * 8, hd), F32),
                pltpu.VMEM((slots * 8, span), F32),
                pltpu.VMEM((slots * 8, hd), F32),
                pltpu.VMEM((8, hd), BF),
                pltpu.VMEM((n, 8, hd), BF),
                pltpu.VMEM((2, half, width), F32),
                pltpu.VMEM((half, width), F32),
                pltpu.VMEM((experts * 2 * cols, hd), F32),
                pltpu.VMEM((experts, 2 * cols, hd), BF),
                pltpu.VMEM((n, 2 * cols, hd), BF),
                pltpu.VMEM((n * 2 * cols, hd), F32),
                pltpu.VMEM((n, 2 * cols, hd), BF),
                pltpu.VMEM((n, 2 * cols, hd), BF),
                pltpu.SMEM(page_table.shape[::-1], jnp.int32),
                pltpu.SMEM(lengths.shape, jnp.int32),
                pltpu.SMEM(new_owner.shape, jnp.int32),
                pltpu.SMEM(routes.shape[::-1], jnp.int32),
                pltpu.VMEM((half, width), F32),
                pltpu.VMEM((3 * half * cols, n * 2 * cols), BF),
                pltpu.VMEM((3 * half * cols, n * 16), BF),
                pltpu.VMEM((1, width), F32),
                pltpu.VMEM((1, width), F32),
                pltpu.VMEM((16, hd), BF),
                pltpu.VMEM((n, 16, hd), BF),
                pltpu.VMEM((16, hd), F32),
                pltpu.VMEM((16, hd), BF),
                pltpu.VMEM((n, 16, hd), BF),
                pltpu.VMEM((n * 16, hd), F32),
                pltpu.VMEM((n, 16, hd), BF),
                pltpu.VMEM((n, 16, hd), BF),
                dma((17,)),
                dma((3,)),
                dma((3,)),
                dma,
                dma,
                dma,
                dma,
                dma((6,)),
                dma((6,)),
            ],
            compiler_params=pltpu.CompilerParams(
                collective_id=0, has_side_effects=True, vmem_limit_bytes=60 * 1024 * 1024
            ),
        )(
            page_table.T,
            lengths,
            new_owner,
            routes.T,
            tokens,
            gain_attn,
            gain_moe,
            w_query,
            w_key,
            w_value,
            w_out,
            cache_k,
            cache_v,
            w_router.T,
            jnp.swapaxes(w_gate, 1, 2),
            jnp.swapaxes(w_up, 1, 2),
            jnp.swapaxes(w_down, 1, 2),
        )

    return jax.shard_map(
        shards,
        mesh=mesh,
        in_specs=(
            P("req", None),
            P(),
            P(None, "kv"),
            P(None, "kv"),
            P(None, "kv"),
            P("kv", None),
            P("req", None, "kv"),
            P("req", None, "kv"),
            P("req", None),
            P(),
            P(),
            P(),
            P(),
            P(("req", "kv"), None),
            P("req", None, "kv"),
            P("req", None, "kv"),
            P("req", None, "kv"),
        ),
        out_specs=P(("req", "kv"), None),
        check_vma=False,
    )
```

```python
import functools
import itertools

import jax
import jax.numpy as jnp
from jax import lax
from jax.experimental import pallas as pl
from jax.experimental.pallas import tpu as pltpu
from jax.sharding import PartitionSpec as P

BF = jnp.bfloat16
F32 = jnp.float32
LAST = (((1,), (1,)), ((), ()))


def rms_scaled(wide, gain_row):
    squares = jnp.mean(wide * wide, axis=-1, keepdims=True)
    return (wide * lax.rsqrt(squares + 1e-06) * gain_row).astype(BF)


def wait_bytes(ref, sem):
    pltpu.make_async_copy(ref, ref, sem).wait()


def layer_kernel(
    n,
    pages_h,
    lengths_h,
    owner_h,
    routes_h,
    tokens_h,
    gain_a_h,
    gain_m_h,
    wq_h,
    wk_h,
    wv_h,
    wo_h,
    ck_h,
    cv_h,
    wr_h,
    wg_h,
    wu_h,
    wd_h,
    out_ref,
    tok,
    gain_a,
    gain_m,
    wqkv,
    wo,
    ck,
    cv,
    wr,
    wg,
    wu,
    wd,
    heads,
    scores,
    att,
    q_out,
    q_in,
    head_sum,
    head_in,
    wide_a,
    disp_out,
    disp_in,
    wide_b,
    ret_out,
    ret_in,
    pages_s,
    lengths_s,
    owner_s,
    routes_s,
    fin,
    row_sum,
    row_in,
    t_out,
    t_in,
    m_wide,
    m_out,
    m_in,
    wide_m,
    late_out,
    late_in,
    load_sems,
    w_send,
    w_recv,
    h_send,
    h_recv,
    r_send,
    r_recv,
    send_sems,
    recv_sems,
):
    me = lax.axis_index("req")
    kv = lax.axis_index("kv")
    slots, width = tok.shape
    half = slots // 2
    hd = ck.shape[2]
    page = ck.shape[1]
    per_slot = pages_s.shape[0]
    groups = wo.shape[0] // hd
    experts = n // 2
    cols = width // hd
    inv_root = hd ** (-0.5)

    side = round(n ** (1 / 3))
    me_z, me_x, me_y = me // (side * side), lax.rem(me // side, side), lax.rem(me, side)
    turn = 1 + (side - 2) * kv
    at_z = [lax.rem(me_z + d * turn, side) * (side * side) for d in range(side)]
    at_x = [lax.rem(me_x + d * turn, side) * side for d in range(side)]
    at_y = [lax.rem(me_y + d * turn, side) for d in range(side)]

    def hops(offset):
        return sum(min(d, side - d) for d in offset)

    offsets = sorted(
        (o for o in itertools.product(range(side), repeat=3) if any(o)), key=lambda o: (-hops(o), o[::-1])
    )

    def shifted(offset):
        dz, dx, dy = offset
        return at_z[dz] + at_x[dx] + at_y[dy]

    sibling = {"kv": 1 - kv}
    relocating = kv == 1
    barrier = pltpu.get_barrier_semaphore()
    for offset in offsets:
        pl.semaphore_signal(barrier, 1, device_id={"req": shifted(offset)})
    pl.semaphore_signal(barrier, 1, device_id=sibling)

    def load(src, dst, i):
        copy = pltpu.make_async_copy(src, dst, load_sems.at[i])
        copy.start()
        return copy

    qcols = wq_h.shape[1]
    l_tok = load(tokens_h, tok, 0)
    l_gain = load(gain_a_h, gain_a, 1)
    l_gain_m = load(gain_m_h, gain_m, 12)
    l_wq = load(wq_h, wqkv.at[:, pl.ds(0, qcols)], 2)
    l_wk = load(wk_h, wqkv.at[:, pl.ds(qcols, hd)], 3)
    l_wv = load(wv_h, wqkv.at[:, pl.ds(qcols + hd, hd)], 4)

    l_ints = [
        load(src, dst, 13 + i)
        for i, (src, dst) in enumerate(
            (
                (pages_h, pages_s),
                (lengths_h, lengths_s),
                (owner_h, owner_s),
                (routes_h, routes_s),
            )
        )
    ]
    l_ck = load(ck_h, ck, 5)
    l_cv = load(cv_h, cv, 6)
    l_wo = load(wo_h, wo, 7)
    l_wr = load(wr_h, wr, 8)
    l_wg = load(wg_h.at[0], wg.at[0], 9)
    l_wu = load(wu_h.at[0], wu.at[0], 10)
    l_wd = load(wd_h.at[0], wd.at[0], 11)

    def to_all(src_of, dst, phase):
        for offset in offsets:
            peer = shifted(offset)
            pltpu.make_async_remote_copy(
                src_ref=src_of(peer),
                dst_ref=dst.at[me],
                send_sem=send_sems.at[phase],
                recv_sem=recv_sems.at[phase],
                device_id={"req": peer},
            ).start()
        pltpu.make_async_copy(src_of(me), dst.at[me], recv_sems.at[phase]).start()

    l_tok.wait()
    l_gain.wait()
    l_gain_m.wait()
    gain_attn = gain_a[...].astype(F32).reshape(1, width)
    gain_moe = gain_m[...].astype(F32).reshape(1, width)
    tokf = tok[...].astype(F32)
    normed = rms_scaled(tokf, gain_attn)
    last = (slots - 1) * 8
    m_wide[...] = jnp.zeros((16, hd), F32)
    for c in range(cols):
        m_wide[c : c + 1, :] = tokf[slots - 1 : slots, c * hd : (c + 1) * hd]
    t_out[...] = m_wide[...].astype(BF)
    l_wq.wait()
    l_wk.wait()
    l_wv.wait()
    qkv = jnp.dot(normed, wqkv[...], preferred_element_type=F32).astype(BF).astype(F32)
    for h in range(groups + 2):
        heads[pl.ds(h, slots, stride=8), :] = qkv[:, h * hd : (h + 1) * hd]
    q_out[...] = heads[last : last + 8, :].astype(BF)
    pl.semaphore_wait(barrier, n)
    to_all(lambda peer: q_out, q_in, 0)

    @pl.when(relocating)
    def _():
        to_all(lambda peer: t_out, t_in, 1)

    def attend(first, count):
        rows = slice(first * 8, (first + count) * 8)
        place = lax.broadcasted_iota(jnp.int32, (8, page), 1)
        for s in range(first, first + count):
            block = heads[s * 8 : s * 8 + 8, :].astype(BF)
            live = lengths_s[me * slots + s]
            for j in range(per_slot):
                dots = lax.dot_general(
                    block, ck[pages_s[j, s]], LAST, preferred_element_type=F32
                )
                scores[s * 8 : s * 8 + 8, j * page : (j + 1) * page] = jnp.where(
                    place + j * page < live, dots * inv_root, -1e30
                )
        all_scores = scores[rows, :]
        top = jnp.max(all_scores, axis=-1, keepdims=True)
        weights = jnp.exp(all_scores - top)
        total = jnp.sum(weights, axis=-1, keepdims=True)
        scores[rows, :] = weights
        for s in range(first, first + count):
            acc = jnp.zeros((8, hd), F32)
            for j in range(per_slot):
                acc = acc + jnp.dot(
                    scores[s * 8 : s * 8 + 8, j * page : (j + 1) * page].astype(BF),
                    cv[pages_s[j, s]],
                    preferred_element_type=F32,
                )
            att[s * 8 : s * 8 + 8, :] = acc
        block = heads[rows, :].reshape(count, 8, hd)
        own = jnp.sum(block * block[:, groups : groups + 1, :], axis=-1, keepdims=True) * inv_root
        top = top.reshape(count, 8, 1)
        total = total.reshape(count, 8, 1)
        joint = jnp.maximum(top, own)
        old_part = jnp.exp(top - joint)
        new_part = jnp.exp(own - joint)
        merged = (
            att[rows, :].reshape(count, 8, hd) * old_part
            + new_part * block[:, groups + 1 : groups + 2, :]
        )
        result = merged / (total * old_part + new_part)
        att[rows, :] = result.astype(BF).astype(F32).reshape(count * 8, hd)

    for l_int in l_ints:
        l_int.wait()
    l_ck.wait()
    l_cv.wait()
    attend(0, slots - 1)
    att[last : last + 8, :] = jnp.zeros((8, hd), F32)
    l_wo.wait()

    def head_terms():
        attended = jnp.concatenate(
            [att[pl.ds(h, slots, stride=8), :].astype(BF) for h in range(groups)], axis=1
        )
        return jnp.dot(attended, wo[...], preferred_element_type=F32)

    terms = head_terms()
    head_sum[0] = terms[:half]
    head_sum[1] = terms[half:]
    cross = pltpu.make_async_remote_copy(
        src_ref=head_sum.at[1 - kv],
        dst_ref=head_in,
        send_sem=h_send,
        recv_sem=h_recv,
        device_id=sibling,
    )
    cross.start()
    first_core = kv == 0
    mine = jnp.where(first_core, terms[:half], terms[half:])
    residual = jnp.where(first_core, tokf[:half], tokf[half:])

    topk = routes_s.shape[0]
    lane = lax.broadcasted_iota(jnp.int32, (half, 128), 1)
    row = lax.broadcasted_iota(jnp.int32, (half, 128), 0)
    late_row = (row == half - 1) & relocating
    route = []
    for j in range(topk):
        named_by = jnp.zeros((half, 128), jnp.int32)
        for i in range(half):
            named_by = jnp.where(row == i, routes_s[j, i], named_by)
        route.append(named_by)
    early = [jnp.where(late_row, -1, r) for r in route]

    def places(expert, slot):
        named = jnp.zeros((half, 128), F32)
        for j in range(topk):
            named = named + jnp.where(early[j] == expert, 1.0, 0.0)
        rank = jnp.zeros((half, 128), F32)
        for i in range(half - 1):
            rank = rank + jnp.where(row > i, named[i : i + 1, :], 0.0)
        return jnp.where(rank == slot.astype(F32), named, 0.0)

    pick = places(lane % experts, lane // experts)
    pick_t = jnp.transpose(pick)[: 2 * experts, :].astype(BF)
    peer_expert = (lane % n) // 2
    peer_place = places(peer_expert, lane // n)

    cross.wait_recv()
    middle = (residual + (mine + head_in[...])).astype(BF).astype(F32)
    normed_two = rms_scaled(middle, gain_moe)
    outgoing = jnp.dot(pick_t, normed_two, preferred_element_type=F32)
    for c in range(cols):
        for k in range(2):
            wide_a[pl.ds(c * 2 + k, experts, stride=2 * cols), :] = outgoing[
                k * experts : (k + 1) * experts, c * hd : (c + 1) * hd
            ]
    disp_out[...] = wide_a[...].reshape(experts, 2 * cols, hd).astype(BF)
    to_all(lambda peer: disp_out.at[peer // 2], disp_in, 2)
    swaps = []
    for i, (src, dst) in enumerate(((wg_h, wg), (wu_h, wu), (wd_h, wd))):
        swap = pltpu.make_async_remote_copy(
            src_ref=src.at[0],
            dst_ref=dst.at[1],
            send_sem=w_send.at[i],
            recv_sem=w_recv.at[i],
            device_id=sibling,
        )
        swap.start()
        swaps.append(swap)

    wait_bytes(q_in, recv_sems.at[0])
    served = owner_s[me]
    heads[last : last + 8, :] = q_in[served].astype(F32)
    attend(slots - 1, 1)
    late_terms = head_terms()[slots - 1 : slots, :]
    row_sum[...] = late_terms

    def row_copy():
        return pltpu.make_async_remote_copy(
            src_ref=row_sum,
            dst_ref=row_in,
            send_sem=r_send,
            recv_sem=r_recv,
            device_id=sibling,
        )

    @pl.when(first_core)
    def _():
        row_copy().start()

    l_wr.wait()

    def route_weights(normed_rows, chosen_by):
        logits = lax.dot_general(normed_rows, wr[...], LAST, preferred_element_type=F32)
        choice = lax.broadcasted_iota(jnp.int32, logits.shape, 1)
        chosen = [
            jnp.sum(jnp.where(choice == r[:, :experts], logits, 0.0), axis=-1, keepdims=True)
            for r in chosen_by
        ]
        best = functools.reduce(jnp.maximum, chosen)
        powers = [jnp.exp(c - best) for c in chosen]
        denom = functools.reduce(jnp.add, powers)
        blend = jnp.zeros((half, 128), F32)
        for r, power in zip(chosen_by, powers):
            blend = blend + jnp.where(r == peer_expert, power / denom, 0.0)
        return blend

    def in_parts(blend):
        part_a = blend.astype(BF).astype(F32)
        part_b = (blend - part_a).astype(BF).astype(F32)
        part_c = blend - part_a - part_b
        return jnp.concatenate([part_a, part_b, part_c], axis=0).astype(BF)

    def blended(parts, rows):
        mixed = jnp.dot(parts, rows, preferred_element_type=F32)
        return mixed[:half] + mixed[half : 2 * half] + mixed[2 * half :]

    blend_parts = in_parts(route_weights(normed_two, early) * peer_place)

    @pl.when(relocating)
    def _():
        wait_bytes(t_in, recv_sems.at[1])
        row_copy().wait_recv()
        total = row_sum[...] + row_in[...]
        for c in range(cols):
            m_wide[c : c + 1, :] = total[:, c * hd : (c + 1) * hd]
        m_out[...] = (t_in[served].astype(F32) + m_wide[...]).astype(BF)
        to_all(lambda peer: m_out, m_in, 3)

    def run_expert(rows):
        result = None
        for t in range(2):
            gate = lax.dot_general(rows, wg[t], LAST, preferred_element_type=F32)
            up = lax.dot_general(rows, wu[t], LAST, preferred_element_type=F32)
            hidden = (jnp.maximum(gate, 0.0) * up).astype(BF)
            part = jnp.dot(hidden, wd[t], preferred_element_type=F32)
            result = part if result is None else result + part
        return result

    def unpack(wide, first, stride):
        return jnp.concatenate(
            [wide[pl.ds(first(c), n, stride=stride), :] for c in range(cols)], axis=1
        )

    def unpack_pair():
        return jnp.concatenate(
            [unpack(wide_b, lambda c: c * 2 + k, 2 * cols).astype(BF) for k in range(2)], axis=0
        )

    owners = jnp.zeros((8, 128), jnp.int32)
    owner_lane = lax.broadcasted_iota(jnp.int32, (8, 128), 1)
    for c in range(n):
        owners = jnp.where(owner_lane == c, owner_s[c], owners)
    slot_row = lax.broadcasted_iota(jnp.int32, (n, n), 0)
    moves = jnp.where(slot_row == owners[0:1, :n], 1.0, 0.0).astype(BF)

    def find(c, found):
        return jnp.where(owner_s[c] == me, c, found)

    origin = lax.fori_loop(0, n, find, 0)
    l_wg.wait()
    l_wu.wait()
    l_wd.wait()
    for swap in swaps:
        swap.wait_recv()
    wait_bytes(disp_in, recv_sems.at[2])
    wide_b[...] = disp_in[...].astype(F32).reshape(n * 2 * cols, hd)
    result = run_expert(unpack_pair())
    for c in range(cols):
        for k in range(2):
            wide_b[pl.ds(c * 2 + k, n, stride=2 * cols), :] = result[
                k * n : (k + 1) * n, c * hd : (c + 1) * hd
            ]
    ret_out[...] = wide_b[...].reshape(n, 2 * cols, hd).astype(BF)
    to_all(lambda peer: ret_out.at[peer], ret_in, 4)

    @pl.when(relocating)
    def _():
        wait_bytes(m_in, recv_sems.at[3])
        wide_m[...] = m_in[...].astype(F32).reshape(n * 16, hd)
        late_normed = rms_scaled(unpack(wide_m, lambda c: c, 16), gain_moe)
        ordered = jnp.dot(moves, late_normed, preferred_element_type=F32).astype(BF)
        late_result = run_expert(ordered)

        late_middle = jnp.concatenate(
            [wide_m[pl.ds(origin * 16 + c, 1), :] for c in range(cols)], axis=1
        )
        late_middle = jnp.broadcast_to(late_middle, (half, width))
        for c in range(cols):
            wide_m[pl.ds(c, n, stride=16), :] = late_result[:, c * hd : (c + 1) * hd]
        late_out[...] = wide_m[...].reshape(n, 16, hd).astype(BF)
        to_all(lambda peer: late_out.at[peer], late_in, 5)
        late_blend = in_parts(
            jnp.where(
                lane < n,
                route_weights(rms_scaled(late_middle, gain_moe), route),
                0.0,
            )[:, :n]
        )
        wait_bytes(late_in, recv_sems.at[5])
        wide_m[...] = late_in[...].astype(F32).reshape(n * 16, hd)
        late = late_middle + blended(late_blend, unpack(wide_m, lambda c: c, 16).astype(BF))
        fin[half - 1 : half, :] = late[half - 1 : half, :]

    wait_bytes(ret_in, recv_sems.at[4])
    wide_b[...] = ret_in[...].astype(F32).reshape(n * 2 * cols, hd)
    done = middle + blended(blend_parts, unpack_pair())
    kept = (lax.broadcasted_iota(jnp.int32, (half, width), 0) == half - 1) & relocating
    out_ref[...] = jnp.where(kept, fin[...], done).astype(BF)

    cross.wait_send()
    for swap in swaps:
        swap.wait_send()
    for phase, ref in ((0, q_in), (2, disp_in), (4, ret_in)):
        wait_bytes(ref.at[pl.ds(0, n - 1)], send_sems.at[phase])

    @pl.when(first_core)
    def _():
        row_copy().wait_send()

    @pl.when(relocating)
    def _():
        for phase, ref in ((1, t_in), (3, m_in), (5, late_in)):
            wait_bytes(ref.at[pl.ds(0, n - 1)], send_sems.at[phase])


def solution(mesh):
    n = mesh.shape["req"]

    def shards(
        tokens,
        gain_attn,
        w_query,
        w_key,
        w_value,
        w_out,
        cache_k,
        cache_v,
        page_table,
        lengths,
        new_owner,
        gain_moe,
        w_router,
        routes,
        w_gate,
        w_up,
        w_down,
    ):
        slots, width = tokens.shape
        half = slots // 2
        hd = w_key.shape[1]
        cols = width // hd
        experts = n // 2
        span = page_table.shape[1] * cache_k.shape[1]
        hidden = w_gate.shape[2]
        hbm = pl.BlockSpec(memory_space=pl.ANY)
        dma = pltpu.SemaphoreType.DMA
        return pl.pallas_call(
            functools.partial(layer_kernel, n),
            out_shape=pltpu.VMEM((half, width), BF),
            in_specs=[hbm] * 4 + [hbm] * 13,
            out_specs=pl.BlockSpec(memory_space=pltpu.VMEM),
            scratch_shapes=[
                pltpu.VMEM((slots, width), BF),
                pltpu.VMEM((width,), BF),
                pltpu.VMEM((width,), BF),
                pltpu.VMEM((width, w_query.shape[1] + 2 * hd), BF),
                pltpu.VMEM(w_out.shape, BF),
                pltpu.VMEM(cache_k.shape, BF),
                pltpu.VMEM(cache_v.shape, BF),
                pltpu.VMEM(w_router.shape[::-1], BF),
                pltpu.VMEM((2, hidden, width), BF),
                pltpu.VMEM((2, hidden, width), BF),
                pltpu.VMEM((2, hidden, width), BF),
                pltpu.VMEM((slots * 8, hd), F32),
                pltpu.VMEM((slots * 8, span), F32),
                pltpu.VMEM((slots * 8, hd), F32),
                pltpu.VMEM((8, hd), BF),
                pltpu.VMEM((n, 8, hd), BF),
                pltpu.VMEM((2, half, width), F32),
                pltpu.VMEM((half, width), F32),
                pltpu.VMEM((experts * 2 * cols, hd), F32),
                pltpu.VMEM((experts, 2 * cols, hd), BF),
                pltpu.VMEM((n, 2 * cols, hd), BF),
                pltpu.VMEM((n * 2 * cols, hd), F32),
                pltpu.VMEM((n, 2 * cols, hd), BF),
                pltpu.VMEM((n, 2 * cols, hd), BF),
                pltpu.SMEM(page_table.shape[::-1], jnp.int32),
                pltpu.SMEM(lengths.shape, jnp.int32),
                pltpu.SMEM(new_owner.shape, jnp.int32),
                pltpu.SMEM(routes.shape[::-1], jnp.int32),
                pltpu.VMEM((half, width), F32),
                pltpu.VMEM((1, width), F32),
                pltpu.VMEM((1, width), F32),
                pltpu.VMEM((16, hd), BF),
                pltpu.VMEM((n, 16, hd), BF),
                pltpu.VMEM((16, hd), F32),
                pltpu.VMEM((16, hd), BF),
                pltpu.VMEM((n, 16, hd), BF),
                pltpu.VMEM((n * 16, hd), F32),
                pltpu.VMEM((n, 16, hd), BF),
                pltpu.VMEM((n, 16, hd), BF),
                dma((17,)),
                dma((3,)),
                dma((3,)),
                dma,
                dma,
                dma,
                dma,
                dma((6,)),
                dma((6,)),
            ],
            compiler_params=pltpu.CompilerParams(
                collective_id=0, has_side_effects=True, vmem_limit_bytes=60 * 1024 * 1024
            ),
        )(
            page_table.T,
            lengths,
            new_owner,
            routes.T,
            tokens,
            gain_attn,
            gain_moe,
            w_query,
            w_key,
            w_value,
            w_out,
            cache_k,
            cache_v,
            w_router.T,
            jnp.swapaxes(w_gate, 1, 2),
            jnp.swapaxes(w_up, 1, 2),
            jnp.swapaxes(w_down, 1, 2),
        )

    return jax.shard_map(
        shards,
        mesh=mesh,
        in_specs=(
            P("req", None),
            P(),
            P(None, "kv"),
            P(None, "kv"),
            P(None, "kv"),
            P("kv", None),
            P("req", None, "kv"),
            P("req", None, "kv"),
            P("req", None),
            P(),
            P(),
            P(),
            P(),
            P(("req", "kv"), None),
            P("req", None, "kv"),
            P("req", None, "kv"),
            P("req", None, "kv"),
        ),
        out_specs=P(("req", "kv"), None),
        check_vma=False,
    )
```
